32 devices in a mesh: comp: 2 (over core), tile: 16 (over z, y, x).
Axes of the slice: x: 2, y: 2, z: 4, core: 2. Of those that a mesh axis runs over, the one named last changes fastest.
Arguments:
- tracer: float32 [2, 16, 4, 64, 1024], P('comp', None, None, 'tile'), may hold values from -6 to 6
- velocity: float32 [2, 2, 4, 64, 1024], P('comp', None, None, 'tile'), may hold values from -0.3 to 0.3
- coupling: float32 [2, 16, 64, 1024], P('comp', None, 'tile'), may hold values from 0.05 to 0.5
- sea_mask: int32 [2, 64, 1024], P('comp', 'tile'), may hold values 0 or 1
- send_rows: int32 [2, 16, 4, 2048], P('comp', 'tile'), may hold values from 0 to 3
- send_cols: int32 [2, 16, 4, 2048], P('comp', 'tile'), may hold values from 0 to 1023
- intersection_near: int32 [2, 8, 64, 1024], P('comp', None, 'tile'), may hold values from 0 to 3
- intersection_slot: int32 [2, 8, 64, 1024], P('comp', None, 'tile'), may hold values from 0 to 2047
- intersection_weight: float32 [2, 8, 64, 1024], P('comp', None, 'tile'), as said below
Outputs:
- tracer_out: float32 [2, 16, 4, 64, 1024], P('comp', None, None, 'tile')
The draws below stay inside these ranges and needn't reach their ends.
Inputs may be any that keep to these rules, and one draw needn't show every extreme that they name: `intersection_weight`: positive, summing to one over the 8 intersections of a cell.
All inputs are finite; a program needn't handle non-finite values. No bound on the sum of `sea_mask` on one device may be relied on, other than what follows from the above.
Results may differ from the reference program's by a relative error of at most 0.000088.
Values sent between devices are 32-bit elements; how exact they have to be, the bound alone decides.
A program may use at most 64 MiB of HBM per device.

```python
import math
import jax
import jax.numpy as jnp
from jax import lax

CX = 4
NY = 1024
TRC = 16
LEV = 4
K = 8
NB = 4
CAP = 2048
NX = 64
N_TILE = 16


def draw_intersection_weight(key, part):
    raw = jax.random.uniform(key, (2, K, NX, NY), jnp.float32, 0.2, 1.0)
    return raw / jnp.sum(raw, axis=1, keepdims=True)


def with_ends(array, stream_key, low, high):
    extent = array.shape
    index_at = [jax.random.randint(jax.random.fold_in(stream_key, axis), (), 0, extent[axis]) for axis in range(len(extent))]
    array = array.at[tuple(index_at)].set(low)
    longest = extent.index(max(extent))
    index_at[longest] = (index_at[longest] + 1) % extent[longest]
    return array.at[tuple(index_at)].set(high)


def level_of(key, shape, cuts, least, top_value):
    def one(axis_at, parts):
        draws = jax.random.uniform(jax.random.fold_in(jax.random.fold_in(key, 6), axis_at), (parts,), jnp.float32, least / len(cuts), top_value / len(cuts))
        return jnp.repeat(jnp.exp(draws), shape[axis_at] // parts).reshape((-1,) + (1,) * (len(shape) - axis_at - 1))

    gain = one(*cuts[0])
    for cut in cuts[1:]:
        gain = gain * one(*cut)
    return gain


def noise(rng, extent, scale, bound, shards=(), dtype=jnp.bfloat16):
    array = jax.random.normal(rng, extent, jnp.float32) * scale
    if len(shards) > 0:
        array = level_of(rng, extent, shards, -0.22, 0.18) * array
    return jnp.clip(array, min=-bound, max=bound).astype(dtype)


def setup_inputs(seed: int = 0) -> dict:
    splits = jax.random.split(jax.random.key(seed), 10)
    return {
        "tracer": noise(splits[0], (2, TRC, LEV, NX, NY), 1.0, 6.0, ((0, 2), (3, 16)), jnp.float32),
        "velocity": jnp.clip(jax.random.uniform(splits[1], (2, 2, LEV, NX, NY), jnp.float32, -0.3, 0.3) * level_of(splits[1], (2, 2, LEV, NX, NY), ((0, 2), (3, 16)), -0.4, 0.0), -0.3, 0.3),
        "coupling": jnp.clip(jnp.exp(math.log(0.5) - 2.3025851 * jax.random.uniform(splits[2], (2, TRC, NX, NY), jnp.float32) ** level_of(splits[2], (2, TRC, NX, NY), ((0, 2), (2, 16)), -0.2, 0.2)), 0.05, 0.5),
        "sea_mask": with_ends((jax.random.randint(splits[3], (2, NX, NY), 0, 4) < 3).astype(jnp.int32), jax.random.fold_in(splits[3], 1), 0, 1),
        "send_rows": with_ends(jax.random.randint(splits[4], (2, N_TILE, NB, CAP), 0, CX), jax.random.fold_in(splits[4], 1), 0, CX - 1).astype(jnp.int32),
        "send_cols": with_ends(jax.random.randint(splits[5], (2, N_TILE, NB, CAP), 0, NY), jax.random.fold_in(splits[5], 1), 0, NY - 1).astype(jnp.int32),
        "intersection_near": with_ends(jax.random.randint(splits[6], (2, K, NX, NY), 0, NB), jax.random.fold_in(splits[6], 1), 0, NB - 1).astype(jnp.int32),
        "intersection_slot": with_ends(jax.random.randint(splits[7], (2, K, NX, NY), 0, CAP), jax.random.fold_in(splits[7], 1), 0, CAP - 1).astype(jnp.int32),
        "intersection_weight": draw_intersection_weight(jax.random.fold_in(splits[9], 71), 0),
    }


diffusion = 0.12


def substep(field, speed):
    east = jnp.roll(field, -1, axis=2)
    west = jnp.roll(field, 1, axis=2)
    north = jnp.roll(field, -1, axis=3)
    south = jnp.roll(field, 1, axis=3)
    return field - 0.5 * speed[0] * (east - west) - 0.5 * speed[1] * (north - south) + diffusion * (east + west + north + south - 4.0 * field)


def reference(tracer, velocity, coupling, sea_mask, send_rows, send_cols, intersection_near, intersection_slot, intersection_weight):
    results = []
    for comp in range(2):
        other = 1 - comp
        surface = tracer[other, :, 0].reshape(TRC, NX * NY)
        xpos = lax.broadcasted_iota(jnp.int32, (NX, NY), 0)
        dest_tile = xpos // CX
        remapped = jnp.zeros((TRC, NX, NY), jnp.float32)
        for k in range(K):
            near = intersection_near[comp, k]
            source = ((dest_tile + near - 1 + N_TILE) % N_TILE).astype(jnp.int32)
            within = intersection_slot[comp, k]
            row_local = send_rows[other][source, near, within]
            col_local = send_cols[other][source, near, within]
            cell = ((source * CX + row_local) * NY + col_local).astype(jnp.int32)
            picked = jnp.take(surface, cell.reshape(-1), axis=1).reshape(TRC, NX, NY)
            remapped = remapped + intersection_weight[comp, k] * picked
        level0 = tracer[comp, :, 0]
        masked = sea_mask[comp].astype(jnp.float32)
        new0 = level0 + coupling[comp] * masked * (remapped - level0)
        field = tracer[comp].at[:, 0].set(new0)
        speed = velocity[comp]
        for step in range(2):
            field = substep(field, speed)
        results.append(field)
    return jnp.stack(results)
```

```python
import functools

import jax
import jax.numpy as jnp
from jax import lax
from jax.experimental import pallas as pl
from jax.experimental.pallas import tpu as pltpu
from jax.sharding import PartitionSpec as P

diffusion = 0.12
LANES = 128
MESH = pl.DeviceIdType.MESH
PAIR = 2
ON_LANES = 2


def lane_pick(table, lanes):
    return jnp.take_along_axis(table, lanes, axis=1, mode="promise_in_bounds")


def pick_blocks(blocks, his, los, tracers):
    halves = tracers // 8
    picked = []
    for hi, lo in zip(his, los):
        chains = [[jnp.zeros((8, LANES), jnp.float32)] * 2 for _ in range(halves)]
        for n, (ident, load) in enumerate(blocks):
            hit = hi == ident
            for half in range(halves):
                chain = chains[half]
                chain[n % 2] = jnp.where(hit, lane_pick(load(half), lo), chain[n % 2])
        picked.append([one + two for one, two in chains])
    return picked


def split_pieces(value, pieces, block, tracers):
    top = value.astype(jnp.bfloat16)
    rest = (value - top.astype(jnp.float32)).astype(jnp.bfloat16)
    rows_at = pl.ds(block * tracers, tracers)
    pieces[rows_at, pl.ds(0, LANES)] = top
    pieces[rows_at, pl.ds(LANES, LANES)] = rest


def dot_blocks(left, his, los, tracers):
    halves = tracers // 8
    count = left.shape[0] // tracers
    lane_id = lax.broadcasted_iota(jnp.int32, (LANES, LANES), 0)
    picked = []
    for k in range(0, len(his), PAIR):
        hots = []
        for lo in los[k : k + PAIR]:
            hot = lane_id == jnp.broadcast_to(lo, (LANES, LANES))
            hot = hot.astype(jnp.float32).astype(jnp.bfloat16)
            hots.append(jnp.concatenate([hot, hot], axis=0))
        found = jnp.dot(
            left, jnp.concatenate(hots, axis=1), preferred_element_type=jnp.float32
        )
        for n, hi in enumerate(his[k : k + PAIR]):
            hi = jnp.broadcast_to(hi, (8, LANES))
            part = [jnp.zeros((8, LANES), jnp.float32)] * halves
            for block in range(count):
                hit = hi == block
                for half in range(halves):
                    row = block * tracers + half * 8
                    cell = found[row : row + 8, n * LANES : (n + 1) * LANES]
                    part[half] = jnp.where(hit, cell, part[half])
            picked.append(part)
    return picked


def exchange_kernel(
    dims,
    tracer_ref,
    vel_ref,
    coup_ref,
    mask_ref,
    rows_ref,
    cols_ref,
    near_ref,
    slot_ref,
    weight_ref,
    out_ref,
    lev_ref,
    vel_buf,
    packed,
    received,
    first,
    pieces,
    surface_pieces,
    pack_send,
    pack_recv,
    field_send,
    field_recv,
    first_send,
    first_recv,
):
    tiles, tracers, levels, rows, chunks, nears, blocks, inters = dims
    groups = rows * chunks
    halves = tracers // 8
    me_c = lax.axis_index("comp")
    me_t = lax.axis_index("tile")
    other = 1 - me_c

    def tile_at(step):
        return lax.rem(me_t + step + tiles, tiles)

    up, down = tile_at(1), tile_at(-1)
    barrier = pltpu.get_barrier_semaphore()
    for j in range(nears):
        pl.semaphore_signal(
            barrier, inc=1, device_id=(other, tile_at(j - 1)), device_id_type=MESH
        )
    for side in (up, down):
        pl.semaphore_signal(barrier, inc=1, device_id=(me_c, side), device_id_type=MESH)

    def load_level(level):
        def one(g, _):
            c, r = g // rows, g % rows
            lev_ref[level, 1 + r, c] = tracer_ref[
                pl.ds(level * groups + g, tracers, stride=levels * groups), :
            ]
            return 0

        lax.fori_loop(0, groups, one, 0)

    load_level(0)

    def wide(ref, row):
        return jnp.broadcast_to(ref[pl.ds(row, 1), :], (8, LANES))

    for r in range(rows):
        for c in range(chunks):
            split_pieces(lev_ref[0, 1 + r, c], surface_pieces, r * chunks + c, tracers)

    def pack(j):
        batch = 8

        def one(b, _):
            his, los = [], []
            for n in range(batch):
                at = (b * batch + n) * nears + j
                row, col = rows_ref[pl.ds(at, 1), :], cols_ref[pl.ds(at, 1), :]
                his.append(row * chunks + (col >> 7))
                los.append(col & 127)
            on_mxu = batch - 2
            picked = dot_blocks(surface_pieces[...], his[:on_mxu], los[:on_mxu], tracers)
            table = [
                (
                    r * chunks + c,
                    lambda half, r=r, c=c: lev_ref[0, 1 + r, c, pl.ds(half * 8, 8), :],
                )
                for r in range(rows)
                for c in range(chunks)
            ]
            picked += pick_blocks(
                table,
                [jnp.broadcast_to(x, (8, LANES)) for x in his[on_mxu:]],
                [jnp.broadcast_to(x, (8, LANES)) for x in los[on_mxu:]],
                tracers,
            )
            for n in range(batch):
                for half in range(halves):
                    packed[j, b * batch + n, pl.ds(half * 8, 8), :] = picked[n][half]
            return 0

        lax.fori_loop(0, blocks // batch, one, 0)

    order = [j for j in range(nears) if j != 1] + [1]
    pack_copies = {}
    for at, j in enumerate(order):
        pack(j)
        if at == 0:
            pl.semaphore_wait(barrier, nears + 2)
        pack_copies[j] = pltpu.make_async_remote_copy(
            src_ref=packed.at[j],
            dst_ref=received.at[j],
            send_sem=pack_send.at[j],
            recv_sem=pack_recv.at[j],
            device_id=(other, tile_at(1 - j)),
            device_id_type=MESH,
        )
        pack_copies[j].start()

    def to_side(ref, sends, recvs, level, side):
        src, dst, target = ((1, rows + 1, down), (rows, 0, up))[side]
        copy = pltpu.make_async_remote_copy(
            src_ref=ref.at[level, src],
            dst_ref=ref.at[level, dst],
            send_sem=sends.at[level, side],
            recv_sem=recvs.at[level, side],
            device_id=(me_c, target),
            device_id_type=MESH,
        )
        copy.start()
        return copy

    field_copies, first_copies = {}, {}
    for level in range(1, levels):
        load_level(level)
        for side in range(2):
            field_copies[level, side] = to_side(
                lev_ref, field_send, field_recv, level, side
            )

    def load_velocity(i, _):
        for c in range(chunks):
            for r in range(rows):
                vel_buf[r, i, c] = vel_ref[pl.ds(i * groups + c * rows + r, 1), :]
        return 0

    lax.fori_loop(0, 2 * levels, load_velocity, 0)

    def remap(r, c):
        g = c * rows + r
        table = [
            (
                j * blocks + b,
                lambda half, j=j, b=b: received[j, b, pl.ds(half * 8, 8), :],
            )
            for j in range(nears)
            for b in range(blocks)
        ]
        his, los, weights = [], [], []
        for k in range(inters):
            at = k * groups + g
            his.append(near_ref[pl.ds(at, 1), :] * blocks + (slot_ref[pl.ds(at, 1), :] >> 7))
            los.append(slot_ref[pl.ds(at, 1), :] & 127)
            weights.append(wide(weight_ref, at))
        on_mxu = inters - ON_LANES
        picked = dot_blocks(pieces[...], his[:on_mxu], los[:on_mxu], tracers)
        if ON_LANES > 0:
            picked += pick_blocks(
                table,
                [jnp.broadcast_to(x, (8, LANES)) for x in his[on_mxu:]],
                [jnp.broadcast_to(x, (8, LANES)) for x in los[on_mxu:]],
                tracers,
            )
        sums = [jnp.zeros((8, LANES), jnp.float32)] * halves
        for weight, part in zip(weights, picked):
            sums = [sums[half] + weight * part[half] for half in range(halves)]
        return sums

    def couple(r, c, sums):
        g = c * rows + r
        mask = wide(mask_ref, g).astype(jnp.float32)
        coup = coup_ref[pl.ds(g, tracers, stride=groups), :]
        for half in range(halves):
            at = pl.ds(half * 8, 8)
            old = lev_ref[0, 1 + r, c, at, :]
            part = coup[half * 8 : half * 8 + 8]
            lev_ref[0, 1 + r, c, at, :] = old + part * mask * (sums[half] - old)

    lane = lax.broadcasted_iota(jnp.int32, (chunks * tracers, LANES), 1)

    def stepped(ref, level, row):
        west, field, east = ref[level, row], ref[level, row + 1], ref[level, row + 2]
        flat = field.reshape(chunks * tracers, LANES)
        ahead = pltpu.roll(flat, LANES - 1, 1)
        behind = pltpu.roll(flat, 1, 1)
        north = jnp.where(
            lane == LANES - 1,
            jnp.concatenate([ahead[tracers:], ahead[:tracers]], axis=0),
            ahead,
        ).reshape(chunks, tracers, LANES)
        south = jnp.where(
            lane == 0,
            jnp.concatenate([behind[-tracers:], behind[:-tracers]], axis=0),
            behind,
        ).reshape(chunks, tracers, LANES)
        u = vel_buf[row, level]
        v = vel_buf[row, levels + level]
        return (
            field
            - 0.5 * u * (east - west)
            - 0.5 * v * (north - south)
            + diffusion * (east + west + north + south - 4.0 * field)
        )

    def step_one(level, row):
        first[level, row + 1] = stepped(lev_ref, level, row)

    def step_two(level, row):
        value = stepped(first, level, row)
        for c in range(chunks):
            at = level * groups + c * rows + row
            out_ref[pl.ds(at, tracers, stride=levels * groups), :] = value[c]

    def each_level(start, fn):
        def one(level, _):
            fn(level)
            return 0

        lax.fori_loop(start, levels, one, 0)

    def inside(step, level):
        def one(row, _):
            step(level, row)
            return 0

        lax.fori_loop(1, rows - 1, one, 0)

    def send_field(level, side):
        field_copies[level, side] = to_side(lev_ref, field_send, field_recv, level, side)

    def send_first(level, side):
        field_copies[level, 1 - side].wait_recv()
        step_one(level, (0, rows - 1)[side])
        first_copies[level, side] = to_side(first, first_send, first_recv, level, side)

    def couple_row(r):
        def one(c, _):
            couple(r, c, remap(r, c))
            return 0

        lax.fori_loop(0, chunks, one, 0, unroll=2)

    each_level(1, lambda level: inside(step_one, level))

    def split_slots(j):
        def one(b, _):
            split_pieces(received[j, b], pieces, j * blocks + b, tracers)
            return 0

        lax.fori_loop(0, blocks, one, 0)

    for j in [1] + order[:-1]:
        pack_copies[j].wait_recv()
        split_slots(j)

    inner = list(range(1, levels))
    couple_row(0)
    send_field(0, 0)
    for level in inner[:1]:
        send_first(level, 0)
        send_first(level, 1)
    couple_row(rows - 1)
    send_field(0, 1)
    for level in inner[1:]:
        send_first(level, 0)
        send_first(level, 1)
    for r in range(1, rows - 1):
        couple_row(r)
        if r == 1:
            send_first(0, 0)
    inside(step_one, 0)
    send_first(0, 1)
    each_level(0, lambda level: inside(step_two, level))
    for level in inner + [0]:
        for side in range(2):
            first_copies[level, 1 - side].wait_recv()
            step_two(level, (0, rows - 1)[side])
    for copy in [*pack_copies.values(), *field_copies.values(), *first_copies.values()]:
        copy.wait_send()


def split_rows(x):
    *lead, rows, width = x.shape
    chunks = width // LANES
    x = jnp.swapaxes(x.reshape(*lead, rows, chunks, LANES), -3, -2)
    return x.reshape(-1, LANES)


def per_device(
    tiles,
    tracer,
    velocity,
    coupling,
    sea_mask,
    send_rows,
    send_cols,
    intersection_near,
    intersection_slot,
    intersection_weight,
):
    _, tracers, levels, rows, width = tracer.shape
    nears, capacity = send_rows.shape[2:]
    inters = intersection_slot.shape[1]
    chunks, blocks = width // LANES, capacity // LANES
    dims = (tiles, tracers, levels, rows, chunks, nears, blocks, inters)
    dma = pltpu.SemaphoreType.DMA
    vmem = pl.BlockSpec(memory_space=pltpu.VMEM)
    f32 = jnp.float32
    out = pl.pallas_call(
        functools.partial(exchange_kernel, dims),
        out_shape=jax.ShapeDtypeStruct((tracers * levels * rows * chunks, LANES), f32),
        in_specs=[vmem] * 9,
        out_specs=vmem,
        scratch_shapes=[
            pltpu.VMEM((levels, rows + 2, chunks, tracers, LANES), f32),
            pltpu.VMEM((rows, 2 * levels, chunks, 1, LANES), f32),
            pltpu.VMEM((nears, blocks, tracers, LANES), f32),
            pltpu.VMEM((nears, blocks, tracers, LANES), f32),
            pltpu.VMEM((levels, rows + 2, chunks, tracers, LANES), f32),
            pltpu.VMEM((nears * blocks * tracers, 2 * LANES), jnp.bfloat16),
            pltpu.VMEM((rows * chunks * tracers, 2 * LANES), jnp.bfloat16),
            dma((nears,)),
            dma((nears,)),
            dma((levels, 2)),
            dma((levels, 2)),
            dma((levels, 2)),
            dma((levels, 2)),
        ],
        compiler_params=pltpu.CompilerParams(collective_id=0, has_side_effects=True),
    )(
        split_rows(tracer),
        split_rows(velocity),
        split_rows(coupling),
        split_rows(sea_mask),
        split_rows(send_rows),
        split_rows(send_cols),
        split_rows(intersection_near),
        split_rows(intersection_slot),
        split_rows(intersection_weight),
    )
    out = out.reshape(1, tracers, levels, chunks, rows, LANES)
    return jnp.swapaxes(out, 3, 4).reshape(tracer.shape)


def solution(mesh):
    in_specs = (
        P("comp", None, None, "tile", None),
        P("comp", None, None, "tile", None),
        P("comp", None, "tile", None),
        P("comp", "tile", None),
        P("comp", "tile", None, None),
        P("comp", "tile", None, None),
        P("comp", None, "tile", None),
        P("comp", None, "tile", None),
        P("comp", None, "tile", None),
    )
    out_specs = P("comp", None, None, "tile", None)
    return jax.shard_map(
        functools.partial(per_device, mesh.shape["tile"]),
        mesh=mesh,
        in_specs=in_specs,
        out_specs=out_specs,
        check_vma=False,
    )
```

```python
import functools

import jax
import jax.numpy as jnp
from jax import lax
from jax.experimental import pallas as pl
from jax.experimental.pallas import tpu as pltpu
from jax.sharding import PartitionSpec as P

diffusion = 0.12
LANES = 128
MESH = pl.DeviceIdType.MESH
PAIR = 2
ON_LANES = 2
ORDER = [0, 2, 3, 1]
EARLY = (1, 2)


def lane_pick(table, lanes):
    return jnp.take_along_axis(table, lanes, axis=1, mode="promise_in_bounds")


def pick_blocks(blocks, his, los, tracers):
    halves = tracers // 8
    picked = []
    for hi, lo in zip(his, los):
        chains = [[jnp.zeros((8, LANES), jnp.float32)] * 2 for _ in range(halves)]
        for n, (ident, load) in enumerate(blocks):
            hit = hi == ident
            for half in range(halves):
                chain = chains[half]
                chain[n % 2] = jnp.where(hit, lane_pick(load(half), lo), chain[n % 2])
        picked.append([one + two for one, two in chains])
    return picked


def split_pieces(value, pieces, block, tracers):
    top = value.astype(jnp.bfloat16)
    rest = (value - top.astype(jnp.float32)).astype(jnp.bfloat16)
    rows_at = pl.ds(block * tracers, tracers)
    pieces[rows_at, pl.ds(0, LANES)] = top
    pieces[rows_at, pl.ds(LANES, LANES)] = rest


def dot_blocks(left, his, los, tracers):
    halves = tracers // 8
    count = left.shape[0] // tracers
    lane_id = lax.broadcasted_iota(jnp.int32, (LANES, LANES), 0)
    picked = []
    for k in range(0, len(his), PAIR):
        hots = []
        for lo in los[k : k + PAIR]:
            hot = lane_id == jnp.broadcast_to(lo, (LANES, LANES))
            hot = hot.astype(jnp.float32).astype(jnp.bfloat16)
            hots.append(jnp.concatenate([hot, hot], axis=0))
        found = jnp.dot(
            left, jnp.concatenate(hots, axis=1), preferred_element_type=jnp.float32
        )
        for n, hi in enumerate(his[k : k + PAIR]):
            hi = jnp.broadcast_to(hi, (8, LANES))
            part = [jnp.zeros((8, LANES), jnp.float32)] * halves
            for block in range(count):
                hit = hi == block
                for half in range(halves):
                    row = block * tracers + half * 8
                    cell = found[row : row + 8, n * LANES : (n + 1) * LANES]
                    part[half] = jnp.where(hit, cell, part[half])
            picked.append(part)
    return picked


def exchange_kernel(
    dims,
    *refs,
):
    sources, refs = refs[:9], refs[9:]
    out_ref, *refs = refs
    (
        lev_ref,
        vel_buf,
        packed,
        received,
        first,
        pieces,
        surface_pieces,
        pack_send,
        pack_recv,
        field_send,
        field_recv,
        first_send,
        first_recv,
        answer,
        input_sem,
        *staged,
    ) = refs
    (
        tracer_ref,
        vel_ref,
        coup_ref,
        mask_ref,
        rows_ref,
        cols_ref,
        near_ref,
        slot_ref,
        weight_ref,
    ) = staged
    tiles, tracers, levels, rows, chunks, nears, blocks, inters = dims
    groups = rows * chunks
    halves = tracers // 8
    me_c = lax.axis_index("comp")
    me_t = lax.axis_index("tile")
    other = 1 - me_c

    def tile_at(step):
        return lax.rem(me_t + step + tiles, tiles)

    up, down = tile_at(1), tile_at(-1)
    inputs = {}
    for n, (source, ref) in enumerate(zip(sources, staged)):
        inputs[n] = pltpu.make_async_copy(source, ref, input_sem.at[n])
        inputs[n].start()

    links = [(other, 1 - j) for j in range(nears)] + [(me_c, 1), (me_c, -1)]
    barrier = pltpu.get_barrier_semaphore()
    awaited = jnp.int32(0)
    for comp, step in links:
        sends_wrap, takes_wrap = me_t + step < 0, me_t - step >= tiles

        @pl.when(jnp.logical_not(takes_wrap))
        def _(comp=comp, step=step):
            pl.semaphore_signal(
                barrier, inc=1, device_id=(comp, tile_at(-step)), device_id_type=MESH
            )

        @pl.when(sends_wrap)
        def _(comp=comp, step=step):
            pl.semaphore_signal(
                barrier, inc=1, device_id=(comp, tile_at(step)), device_id_type=MESH
            )

        awaited += jnp.where(sends_wrap, 0, 1) + jnp.where(takes_wrap, 1, 0)

    def enter():
        pl.semaphore_wait(barrier, awaited)
        for n, (comp, step) in enumerate(links):

            @pl.when(me_t - step >= tiles)
            def _(n=n, comp=comp, step=step):
                pl.semaphore_signal(
                    answer.at[n],
                    inc=1,
                    device_id=(comp, tile_at(-step)),
                    device_id_type=MESH,
                )

    def load_level(level):
        def one(g, _):
            c, r = g // rows, g % rows
            lev_ref[level, 1 + r, c] = tracer_ref[
                pl.ds(level * groups + g, tracers, stride=levels * groups), :
            ]
            return 0

        lax.fori_loop(0, groups, one, 0)

    for n in (0, 4, 5):
        inputs[n].wait()
    load_level(0)

    def wide(ref, row):
        return jnp.broadcast_to(ref[pl.ds(row, 1), :], (8, LANES))

    for r in range(rows):
        for c in range(chunks):
            split_pieces(lev_ref[0, 1 + r, c], surface_pieces, r * chunks + c, tracers)

    def pack(j):
        batch = 8

        def one(b, _):
            his, los = [], []
            for n in range(batch):
                at = (b * batch + n) * nears + j
                row, col = rows_ref[pl.ds(at, 1), :], cols_ref[pl.ds(at, 1), :]
                his.append(row * chunks + (col >> 7))
                los.append(col & 127)
            on_mxu = batch - 2
            picked = dot_blocks(surface_pieces[...], his[:on_mxu], los[:on_mxu], tracers)
            table = [
                (
                    r * chunks + c,
                    lambda half, r=r, c=c: lev_ref[0, 1 + r, c, pl.ds(half * 8, 8), :],
                )
                for r in range(rows)
                for c in range(chunks)
            ]
            picked += pick_blocks(
                table,
                [jnp.broadcast_to(x, (8, LANES)) for x in his[on_mxu:]],
                [jnp.broadcast_to(x, (8, LANES)) for x in los[on_mxu:]],
                tracers,
            )
            for n in range(batch):
                for half in range(halves):
                    packed[j, b * batch + n, pl.ds(half * 8, 8), :] = picked[n][half]
            return 0

        lax.fori_loop(0, blocks // batch, one, 0)

    late = []

    def start(copy, link):
        step = links[link][1]
        if step >= 0:
            copy.start()
            return
        wraps = me_t + step < 0
        pl.when(jnp.logical_not(wraps))(copy.start)
        late.append((link, wraps, copy))

    def start_late():
        for link in sorted({link for link, _, _ in late}):

            @pl.when(me_t + links[link][1] < 0)
            def _(link=link):
                pl.semaphore_wait(answer.at[link], 1)
                for at, _, copy in late:
                    if at == link:
                        copy.start()

        late.clear()

    order = ORDER
    pack_copies = {}
    for at, j in enumerate(order):
        pack(j)
        if at == 0:
            enter()
        pack_copies[j] = pltpu.make_async_remote_copy(
            src_ref=packed.at[j],
            dst_ref=received.at[j],
            send_sem=pack_send.at[j],
            recv_sem=pack_recv.at[j],
            device_id=(other, tile_at(1 - j)),
            device_id_type=MESH,
        )
        start(pack_copies[j], j)

    def to_side(ref, sends, recvs, level, side, opened=True):
        src, dst, target = ((1, rows + 1, down), (rows, 0, up))[side]
        copy = pltpu.make_async_remote_copy(
            src_ref=ref.at[level, src],
            dst_ref=ref.at[level, dst],
            send_sem=sends.at[level, side],
            recv_sem=recvs.at[level, side],
            device_id=(me_c, target),
            device_id_type=MESH,
        )
        if not opened:
            start(copy, nears + 1 - side)
        else:
            copy.start()
        return copy

    field_copies, first_copies = {}, {}
    for level in range(1, levels):
        load_level(level)
        if level in EARLY:
            for side in (1, 0):
                field_copies[level, side] = to_side(
                    lev_ref, field_send, field_recv, level, side, False
                )

    def load_velocity(i, _):
        for c in range(chunks):
            for r in range(rows):
                vel_buf[r, i, c] = vel_ref[pl.ds(i * groups + c * rows + r, 1), :]
        return 0

    for n in (1, 2, 3, 6, 7, 8):
        inputs[n].wait()
    lax.fori_loop(0, 2 * levels, load_velocity, 0)

    def remap(r, c):
        g = c * rows + r
        table = [
            (
                j * blocks + b,
                lambda half, j=j, b=b: received[j, b, pl.ds(half * 8, 8), :],
            )
            for j in range(nears)
            for b in range(blocks)
        ]
        his, los, weights = [], [], []
        for k in range(inters):
            at = k * groups + g
            his.append(near_ref[pl.ds(at, 1), :] * blocks + (slot_ref[pl.ds(at, 1), :] >> 7))
            los.append(slot_ref[pl.ds(at, 1), :] & 127)
            weights.append(wide(weight_ref, at))
        on_mxu = inters - ON_LANES
        picked = dot_blocks(pieces[...], his[:on_mxu], los[:on_mxu], tracers)
        if ON_LANES > 0:
            picked += pick_blocks(
                table,
                [jnp.broadcast_to(x, (8, LANES)) for x in his[on_mxu:]],
                [jnp.broadcast_to(x, (8, LANES)) for x in los[on_mxu:]],
                tracers,
            )
        sums = [jnp.zeros((8, LANES), jnp.float32)] * halves
        for weight, part in zip(weights, picked):
            sums = [sums[half] + weight * part[half] for half in range(halves)]
        return sums

    def couple(r, c, sums):
        g = c * rows + r
        mask = wide(mask_ref, g).astype(jnp.float32)
        coup = coup_ref[pl.ds(g, tracers, stride=groups), :]
        for half in range(halves):
            at = pl.ds(half * 8, 8)
            old = lev_ref[0, 1 + r, c, at, :]
            part = coup[half * 8 : half * 8 + 8]
            lev_ref[0, 1 + r, c, at, :] = old + part * mask * (sums[half] - old)

    lane = lax.broadcasted_iota(jnp.int32, (chunks * tracers, LANES), 1)

    def stepped(ref, level, row):
        west, field, east = ref[level, row], ref[level, row + 1], ref[level, row + 2]
        flat = field.reshape(chunks * tracers, LANES)
        ahead = pltpu.roll(flat, LANES - 1, 1)
        behind = pltpu.roll(flat, 1, 1)
        north = jnp.where(
            lane == LANES - 1,
            jnp.concatenate([ahead[tracers:], ahead[:tracers]], axis=0),
            ahead,
        ).reshape(chunks, tracers, LANES)
        south = jnp.where(
            lane == 0,
            jnp.concatenate([behind[-tracers:], behind[:-tracers]], axis=0),
            behind,
        ).reshape(chunks, tracers, LANES)
        u = vel_buf[row, level]
        v = vel_buf[row, levels + level]
        return (
            field
            - 0.5 * u * (east - west)
            - 0.5 * v * (north - south)
            + diffusion * (east + west + north + south - 4.0 * field)
        )

    def step_one(level, row):
        first[level, row + 1] = stepped(lev_ref, level, row)

    def step_two(level, row):
        value = stepped(first, level, row)
        for c in range(chunks):
            at = level * groups + c * rows + row
            out_ref[pl.ds(at, tracers, stride=levels * groups), :] = value[c]

    def each_level(start, fn):
        def one(level, _):
            fn(level)
            return 0

        lax.fori_loop(start, levels, one, 0)

    def inside(step, level):
        def one(row, _):
            step(level, row)
            return 0

        lax.fori_loop(1, rows - 1, one, 0)

    def send_field(level, side):
        field_copies[level, side] = to_side(lev_ref, field_send, field_recv, level, side)

    def send_first(level, side):
        field_copies[level, 1 - side].wait_recv()
        step_one(level, (0, rows - 1)[side])
        first_copies[level, side] = to_side(first, first_send, first_recv, level, side)

    def couple_row(r):
        def one(c, _):
            couple(r, c, remap(r, c))
            return 0

        lax.fori_loop(0, chunks, one, 0, unroll=2)

    each_level(1, lambda level: inside(step_one, level))
    start_late()

    def split_slots(j):
        def one(b, _):
            split_pieces(received[j, b], pieces, j * blocks + b, tracers)
            return 0

        lax.fori_loop(0, blocks, one, 0)

    for j in [1] + [j for j in order if j != 1]:
        pack_copies[j].wait_recv()
        split_slots(j)

    inner = list(range(1, levels))
    for level in inner:
        if level not in EARLY:
            for side in (1, 0):
                send_field(level, side)
    couple_row(rows - 1)
    send_field(0, 1)
    for level in inner[:1]:
        send_first(level, 1)
        send_first(level, 0)
    couple_row(0)
    send_field(0, 0)
    for level in inner[1:]:
        send_first(level, 1)
        send_first(level, 0)
    for r in reversed(range(1, rows - 1)):
        couple_row(r)
        if r == rows - 2:
            send_first(0, 1)
    inside(step_one, 0)
    send_first(0, 0)
    each_level(0, lambda level: inside(step_two, level))
    for level in inner + [0]:
        for side in (1, 0):
            first_copies[level, 1 - side].wait_recv()
            step_two(level, (0, rows - 1)[side])
    for copy in [*pack_copies.values(), *field_copies.values(), *first_copies.values()]:
        copy.wait_send()


def split_rows(x):
    *lead, rows, width = x.shape
    chunks = width // LANES
    x = jnp.swapaxes(x.reshape(*lead, rows, chunks, LANES), -3, -2)
    return x.reshape(-1, LANES)


def per_device(
    tiles,
    tracer,
    velocity,
    coupling,
    sea_mask,
    send_rows,
    send_cols,
    intersection_near,
    intersection_slot,
    intersection_weight,
):
    _, tracers, levels, rows, width = tracer.shape
    nears, capacity = send_rows.shape[2:]
    inters = intersection_slot.shape[1]
    chunks, blocks = width // LANES, capacity // LANES
    dims = (tiles, tracers, levels, rows, chunks, nears, blocks, inters)
    dma = pltpu.SemaphoreType.DMA
    vmem = pl.BlockSpec(memory_space=pltpu.VMEM)
    f32 = jnp.float32
    operands = [
        split_rows(x)
        for x in (
            tracer,
            velocity,
            coupling,
            sea_mask,
            send_rows,
            send_cols,
            intersection_near,
            intersection_slot,
            intersection_weight,
        )
    ]
    out = pl.pallas_call(
        functools.partial(exchange_kernel, dims),
        out_shape=pltpu.VMEM((tracers * levels * rows * chunks, LANES), f32),
        in_specs=[pl.BlockSpec(memory_space=pltpu.HBM)] * 9,
        out_specs=vmem,
        scratch_shapes=[
            pltpu.VMEM((levels, rows + 2, chunks, tracers, LANES), f32),
            pltpu.VMEM((rows, 2 * levels, chunks, 1, LANES), f32),
            pltpu.VMEM((nears, blocks, tracers, LANES), f32),
            pltpu.VMEM((nears, blocks, tracers, LANES), f32),
            pltpu.VMEM((levels, rows + 2, chunks, tracers, LANES), f32),
            pltpu.VMEM((nears * blocks * tracers, 2 * LANES), jnp.bfloat16),
            pltpu.VMEM((rows * chunks * tracers, 2 * LANES), jnp.bfloat16),
            dma((nears,)),
            dma((nears,)),
            dma((levels, 2)),
            dma((levels, 2)),
            dma((levels, 2)),
            dma((levels, 2)),
            pltpu.SemaphoreType.REGULAR((nears + 2,)),
            dma((len(operands),)),
            *[pltpu.VMEM(x.shape, x.dtype) for x in operands],
        ],
        compiler_params=pltpu.CompilerParams(collective_id=0, has_side_effects=True),
    )(*operands)
    out = out.reshape(1, tracers, levels, chunks, rows, LANES)
    return jnp.swapaxes(out, 3, 4).reshape(tracer.shape)


def solution(mesh):
    in_specs = (
        P("comp", None, None, "tile", None),
        P("comp", None, None, "tile", None),
        P("comp", None, "tile", None),
        P("comp", "tile", None),
        P("comp", "tile", None, None),
        P("comp", "tile", None, None),
        P("comp", None, "tile", None),
        P("comp", None, "tile", None),
        P("comp", None, "tile", None),
    )
    out_specs = P("comp", None, None, "tile", None)
    return jax.shard_map(
        functools.partial(per_device, mesh.shape["tile"]),
        mesh=mesh,
        in_specs=in_specs,
        out_specs=out_specs,
        check_vma=False,
    )
```

```python
import functools

import jax
import jax.numpy as jnp
from jax import lax
from jax.experimental import pallas as pl
from jax.experimental.pallas import tpu as pltpu
from jax.sharding import PartitionSpec as P

diffusion = 0.12
LANES = 128
MESH = pl.DeviceIdType.MESH
PAIR = 2
ON_LANES = (6, 6)
PARTS = ((1,), (0, 2, 3))
GROUP = 2
ORDER = [0, 2, 3, 1]
EARLY = (1, 2, 3)


def lane_pick(table, lanes):
    return jnp.take_along_axis(table, lanes, axis=1, mode="promise_in_bounds")


def pick_blocks(blocks, his, los, tracers):
    halves = tracers // 8
    picked = []
    for hi, lo in zip(his, los):
        chains = [[jnp.zeros((8, LANES), jnp.float32)] * 2 for _ in range(halves)]
        for n, (ident, load) in enumerate(blocks):
            hit = hi == ident
            for half in range(halves):
                chain = chains[half]
                chain[n % 2] = jnp.where(hit, lane_pick(load(half), lo), chain[n % 2])
        picked.append([one + two for one, two in chains])
    return picked


def split_pieces(value, pieces, block, tracers):
    top = value.astype(jnp.bfloat16)
    rest = (value - top.astype(jnp.float32)).astype(jnp.bfloat16)
    rows_at = pl.ds(block * tracers, tracers)
    pieces[rows_at, pl.ds(0, LANES)] = top
    pieces[rows_at, pl.ds(LANES, LANES)] = rest


def dot_blocks(left, idents, his, los, tracers):
    halves = tracers // 8
    lane_id = lax.broadcasted_iota(jnp.int32, (LANES, LANES), 0)
    picked = []
    for k in range(0, len(his), PAIR):
        hots = []
        for lo in los[k : k + PAIR]:
            hot = lane_id == jnp.broadcast_to(lo, (LANES, LANES))
            hot = hot.astype(jnp.float32).astype(jnp.bfloat16)
            hots.append(jnp.concatenate([hot, hot], axis=0))
        found = jnp.dot(
            left, jnp.concatenate(hots, axis=1), preferred_element_type=jnp.float32
        )
        for n, hi in enumerate(his[k : k + PAIR]):
            hi = jnp.broadcast_to(hi, (8, LANES))
            part = [jnp.zeros((8, LANES), jnp.float32)] * halves
            for block, ident in enumerate(idents):
                hit = hi == ident
                for half in range(halves):
                    row = block * tracers + half * 8
                    cell = found[row : row + 8, n * LANES : (n + 1) * LANES]
                    part[half] = jnp.where(hit, cell, part[half])
            picked.append(part)
    return picked


def exchange_kernel(
    dims,
    *refs,
):
    sources, refs = refs[:9], refs[9:]
    out_ref, *refs = refs
    (
        lev_ref,
        vel_buf,
        packed,
        received,
        remapped,
        first,
        pieces,
        surface_pieces,
        pack_send,
        pack_recv,
        field_send,
        field_recv,
        first_send,
        first_recv,
        answer,
        input_sem,
        *staged,
    ) = refs
    (
        tracer_ref,
        vel_ref,
        coup_ref,
        mask_ref,
        rows_ref,
        cols_ref,
        near_ref,
        slot_ref,
        weight_ref,
    ) = staged
    tiles, tracers, levels, rows, chunks, nears, blocks, inters = dims
    groups = rows * chunks
    halves = tracers // 8
    me_c = lax.axis_index("comp")
    me_t = lax.axis_index("tile")
    other = 1 - me_c

    def tile_at(step):
        return lax.rem(me_t + step + tiles, tiles)

    up, down = tile_at(1), tile_at(-1)
    inputs = {}
    for n, (source, ref) in enumerate(zip(sources, staged)):
        inputs[n] = pltpu.make_async_copy(source, ref, input_sem.at[n])
        inputs[n].start()

    links = [(other, 1 - j) for j in range(nears)] + [(me_c, 1), (me_c, -1)]
    barrier = pltpu.get_barrier_semaphore()
    awaited = jnp.int32(0)
    for comp, step in links:
        sends_wrap, takes_wrap = me_t + step < 0, me_t - step >= tiles

        @pl.when(jnp.logical_not(takes_wrap))
        def _(comp=comp, step=step):
            pl.semaphore_signal(
                barrier, inc=1, device_id=(comp, tile_at(-step)), device_id_type=MESH
            )

        @pl.when(sends_wrap)
        def _(comp=comp, step=step):
            pl.semaphore_signal(
                barrier, inc=1, device_id=(comp, tile_at(step)), device_id_type=MESH
            )

        awaited += jnp.where(sends_wrap, 0, 1) + jnp.where(takes_wrap, 1, 0)

    def enter():
        pl.semaphore_wait(barrier, awaited)
        for n, (comp, step) in enumerate(links):

            @pl.when(me_t - step >= tiles)
            def _(n=n, comp=comp, step=step):
                pl.semaphore_signal(
                    answer.at[n],
                    inc=1,
                    device_id=(comp, tile_at(-step)),
                    device_id_type=MESH,
                )

    def load_level(level):
        def one(g, _):
            c, r = g // rows, g % rows
            lev_ref[level, 1 + r, c] = tracer_ref[
                pl.ds(level * groups + g, tracers, stride=levels * groups), :
            ]
            return 0

        lax.fori_loop(0, groups, one, 0)

    for n in (0, 4, 5):
        inputs[n].wait()
    load_level(0)

    def wide(ref, row):
        return jnp.broadcast_to(ref[pl.ds(row, 1), :], (8, LANES))

    for r in range(rows):
        for c in range(chunks):
            split_pieces(lev_ref[0, 1 + r, c], surface_pieces, r * chunks + c, tracers)

    def pack(j):
        batch = 8

        def one(b, _):
            his, los = [], []
            for n in range(batch):
                at = (b * batch + n) * nears + j
                row, col = rows_ref[pl.ds(at, 1), :], cols_ref[pl.ds(at, 1), :]
                his.append(row * chunks + (col >> 7))
                los.append(col & 127)
            on_mxu = batch - 2
            picked = dot_blocks(
                surface_pieces[...],
                range(rows * chunks),
                his[:on_mxu],
                los[:on_mxu],
                tracers,
            )
            table = [
                (
                    r * chunks + c,
                    lambda half, r=r, c=c: lev_ref[0, 1 + r, c, pl.ds(half * 8, 8), :],
                )
                for r in range(rows)
                for c in range(chunks)
            ]
            picked += pick_blocks(
                table,
                [jnp.broadcast_to(x, (8, LANES)) for x in his[on_mxu:]],
                [jnp.broadcast_to(x, (8, LANES)) for x in los[on_mxu:]],
                tracers,
            )
            for n in range(batch):
                for half in range(halves):
                    packed[j, b * batch + n, pl.ds(half * 8, 8), :] = picked[n][half]
            return 0

        lax.fori_loop(0, blocks // batch, one, 0)

    late = []

    def start(copy, link):
        step = links[link][1]
        if step >= 0:
            copy.start()
            return
        wraps = me_t + step < 0
        pl.when(jnp.logical_not(wraps))(copy.start)
        late.append((link, wraps, copy))

    def start_late():
        for link in sorted({link for link, _, _ in late}):

            @pl.when(me_t + links[link][1] < 0)
            def _(link=link):
                pl.semaphore_wait(answer.at[link], 1)
                for at, _, copy in late:
                    if at == link:
                        copy.start()

        late.clear()

    order = ORDER
    pack_copies = {}
    for at, j in enumerate(order):
        pack(j)
        if at == 0:
            enter()
        pack_copies[j] = pltpu.make_async_remote_copy(
            src_ref=packed.at[j],
            dst_ref=received.at[j],
            send_sem=pack_send.at[j],
            recv_sem=pack_recv.at[j],
            device_id=(other, tile_at(1 - j)),
            device_id_type=MESH,
        )
        start(pack_copies[j], j)

    def to_side(ref, sends, recvs, level, side, opened=True):
        src, dst, target = ((1, rows + 1, down), (rows, 0, up))[side]
        copy = pltpu.make_async_remote_copy(
            src_ref=ref.at[level, src],
            dst_ref=ref.at[level, dst],
            send_sem=sends.at[level, side],
            recv_sem=recvs.at[level, side],
            device_id=(me_c, target),
            device_id_type=MESH,
        )
        if not opened:
            start(copy, nears + 1 - side)
        else:
            copy.start()
        return copy

    field_copies, first_copies = {}, {}
    for level in range(1, levels):
        load_level(level)
        if level in EARLY:
            for side in (1, 0):
                field_copies[level, side] = to_side(
                    lev_ref, field_send, field_recv, level, side, False
                )

    def load_velocity(i, _):
        for c in range(chunks):
            for r in range(rows):
                vel_buf[r, i, c] = vel_ref[pl.ds(i * groups + c * rows + r, 1), :]
        return 0

    for n in (1, 2, 3, 6, 7, 8):
        inputs[n].wait()
    lax.fori_loop(0, 2 * levels, load_velocity, 0)

    def remap(r, cs, part):
        places = [(j, b) for j in PARTS[part] for b in range(blocks)]
        idents = [j * blocks + b for j, b in places]
        table = [
            (
                j * blocks + b,
                lambda half, j=j, b=b: received[j, b, pl.ds(half * 8, 8), :],
            )
            for j, b in places
        ]
        before = sum(len(js) for js in PARTS[:part]) * blocks * tracers
        left = pieces[pl.ds(before, len(places) * tracers), :]
        his, los, weights = [], [], []
        for c in cs:
            for k in range(inters):
                at = k * groups + c * rows + r
                slot = slot_ref[pl.ds(at, 1), :]
                his.append(near_ref[pl.ds(at, 1), :] * blocks + (slot >> 7))
                los.append(slot & 127)
                weights.append(wide(weight_ref, at))
        on_mxu = len(his) - ON_LANES[part]
        picked = dot_blocks(left, idents, his[:on_mxu], los[:on_mxu], tracers)
        picked += pick_blocks(
            table,
            [jnp.broadcast_to(x, (8, LANES)) for x in his[on_mxu:]],
            [jnp.broadcast_to(x, (8, LANES)) for x in los[on_mxu:]],
            tracers,
        )
        for n, c in enumerate(cs):
            if part == 0:
                sums = [jnp.zeros((8, LANES), jnp.float32)] * halves
            else:
                sums = [remapped[r, c, pl.ds(half * 8, 8), :] for half in range(halves)]
            for k in range(n * inters, (n + 1) * inters):
                sums = [
                    sums[half] + weights[k] * picked[k][half] for half in range(halves)
                ]
            if part == len(PARTS) - 1:
                couple(r, c, sums)
            else:
                for half in range(halves):
                    remapped[r, c, pl.ds(half * 8, 8), :] = sums[half]

    def couple(r, c, sums):
        g = c * rows + r
        mask = wide(mask_ref, g).astype(jnp.float32)
        coup = coup_ref[pl.ds(g, tracers, stride=groups), :]
        for half in range(halves):
            at = pl.ds(half * 8, 8)
            old = lev_ref[0, 1 + r, c, at, :]
            part = coup[half * 8 : half * 8 + 8]
            lev_ref[0, 1 + r, c, at, :] = old + part * mask * (sums[half] - old)

    lane = lax.broadcasted_iota(jnp.int32, (chunks * tracers, LANES), 1)

    def stepped(ref, level, row):
        west, field, east = ref[level, row], ref[level, row + 1], ref[level, row + 2]
        flat = field.reshape(chunks * tracers, LANES)
        ahead = pltpu.roll(flat, LANES - 1, 1)
        behind = pltpu.roll(flat, 1, 1)
        north = jnp.where(
            lane == LANES - 1,
            jnp.concatenate([ahead[tracers:], ahead[:tracers]], axis=0),
            ahead,
        ).reshape(chunks, tracers, LANES)
        south = jnp.where(
            lane == 0,
            jnp.concatenate([behind[-tracers:], behind[:-tracers]], axis=0),
            behind,
        ).reshape(chunks, tracers, LANES)
        u = vel_buf[row, level]
        v = vel_buf[row, levels + level]
        return (
            field
            - 0.5 * u * (east - west)
            - 0.5 * v * (north - south)
            + diffusion * (east + west + north + south - 4.0 * field)
        )

    def step_one(level, row):
        first[level, row + 1] = stepped(lev_ref, level, row)

    def step_two(level, row):
        value = stepped(first, level, row)
        for c in range(chunks):
            at = level * groups + c * rows + row
            out_ref[pl.ds(at, tracers, stride=levels * groups), :] = value[c]

    def each_level(start, fn):
        def one(level, _):
            fn(level)
            return 0

        lax.fori_loop(start, levels, one, 0)

    def inside(step, level):
        def one(row, _):
            step(level, row)
            return 0

        lax.fori_loop(1, rows - 1, one, 0)

    def send_field(level, side):
        field_copies[level, side] = to_side(lev_ref, field_send, field_recv, level, side)

    def send_first(level, side):
        field_copies[level, 1 - side].wait_recv()
        step_one(level, (0, rows - 1)[side])
        first_copies[level, side] = to_side(first, first_send, first_recv, level, side)

    def gather_row(r, part):
        def one(n, _):
            remap(r, [n * GROUP + i for i in range(GROUP)], part)
            return 0

        lax.fori_loop(0, chunks // GROUP, one, 0, unroll=1)

    def couple_row(r):
        gather_row(r, len(PARTS) - 1)

    each_level(1, lambda level: inside(step_one, level))
    start_late()

    def split_slots(place, j):
        def one(b, _):
            split_pieces(received[j, b], pieces, place * blocks + b, tracers)
            return 0

        lax.fori_loop(0, blocks, one, 0)

    place = 0
    for part, some in enumerate(PARTS):
        for j in some:
            pack_copies[j].wait_recv()
            split_slots(place, j)
            place += 1
        if part < len(PARTS) - 1:

            def one_row(r, _, part=part):
                gather_row(r, part)
                return 0

            lax.fori_loop(0, rows, one_row, 0)

    inner = list(range(1, levels))

    def inner_firsts(some):
        for level in some:
            for side in (1, 0):
                send_first(level, side)

    for level in inner:
        if level not in EARLY:
            for side in (1, 0):
                send_field(level, side)
    couple_row(rows - 1)
    send_field(0, 1)
    inner_firsts(inner[:1])
    couple_row(0)
    send_field(0, 0)
    inner_firsts(inner[1:])
    for r in reversed(range(1, rows - 1)):
        couple_row(r)
        if r == rows - 2:
            send_first(0, 1)
    inside(step_one, 0)
    send_first(0, 0)
    each_level(0, lambda level: inside(step_two, level))
    for level in inner + [0]:
        for side in (1, 0):
            first_copies[level, 1 - side].wait_recv()
            step_two(level, (0, rows - 1)[side])
    for copy in [*pack_copies.values(), *field_copies.values(), *first_copies.values()]:
        copy.wait_send()


def split_rows(x):
    *lead, rows, width = x.shape
    chunks = width // LANES
    x = jnp.swapaxes(x.reshape(*lead, rows, chunks, LANES), -3, -2)
    return x.reshape(-1, LANES)


def per_device(
    tiles,
    tracer,
    velocity,
    coupling,
    sea_mask,
    send_rows,
    send_cols,
    intersection_near,
    intersection_slot,
    intersection_weight,
):
    _, tracers, levels, rows, width = tracer.shape
    nears, capacity = send_rows.shape[2:]
    inters = intersection_slot.shape[1]
    chunks, blocks = width // LANES, capacity // LANES
    dims = (tiles, tracers, levels, rows, chunks, nears, blocks, inters)
    dma = pltpu.SemaphoreType.DMA
    vmem = pl.BlockSpec(memory_space=pltpu.VMEM)
    f32 = jnp.float32
    operands = [
        split_rows(x)
        for x in (
            tracer,
            velocity,
            coupling,
            sea_mask,
            send_rows,
            send_cols,
            intersection_near,
            intersection_slot,
            intersection_weight,
        )
    ]
    out = pl.pallas_call(
        functools.partial(exchange_kernel, dims),
        out_shape=pltpu.VMEM((tracers * levels * rows * chunks, LANES), f32),
        in_specs=[pl.BlockSpec(memory_space=pltpu.HBM)] * 9,
        out_specs=vmem,
        scratch_shapes=[
            pltpu.VMEM((levels, rows + 2, chunks, tracers, LANES), f32),
            pltpu.VMEM((rows, 2 * levels, chunks, 1, LANES), f32),
            pltpu.VMEM((nears, blocks, tracers, LANES), f32),
            pltpu.VMEM((nears, blocks, tracers, LANES), f32),
            pltpu.VMEM((rows, chunks, tracers, LANES), f32),
            pltpu.VMEM((levels, rows + 2, chunks, tracers, LANES), f32),
            pltpu.VMEM((nears * blocks * tracers, 2 * LANES), jnp.bfloat16),
            pltpu.VMEM((rows * chunks * tracers, 2 * LANES), jnp.bfloat16),
            dma((nears,)),
            dma((nears,)),
            dma((levels, 2)),
            dma((levels, 2)),
            dma((levels, 2)),
            dma((levels, 2)),
            pltpu.SemaphoreType.REGULAR((nears + 2,)),
            dma((len(operands),)),
            *[pltpu.VMEM(x.shape, x.dtype) for x in operands],
        ],
        compiler_params=pltpu.CompilerParams(collective_id=0, has_side_effects=True),
    )(*operands)
    out = out.reshape(1, tracers, levels, chunks, rows, LANES)
    return jnp.swapaxes(out, 3, 4).reshape(tracer.shape)


def solution(mesh):
    in_specs = (
        P("comp", None, None, "tile", None),
        P("comp", None, None, "tile", None),
        P("comp", None, "tile", None),
        P("comp", "tile", None),
        P("comp", "tile", None, None),
        P("comp", "tile", None, None),
        P("comp", None, "tile", None),
        P("comp", None, "tile", None),
        P("comp", None, "tile", None),
    )
    out_specs = P("comp", None, None, "tile", None)
    return jax.shard_map(
        functools.partial(per_device, mesh.shape["tile"]),
        mesh=mesh,
        in_specs=in_specs,
        out_specs=out_specs,
        check_vma=False,
    )
```

```python
import functools

import jax
import jax.numpy as jnp
from jax import lax
from jax.experimental import pallas as pl
from jax.experimental.pallas import tpu as pltpu
from jax.sharding import PartitionSpec as P

diffusion = 0.12
LANES = 128
MESH = pl.DeviceIdType.MESH
PAIR = 2
ON_LANES = (6, 6)
PARTS = ((1,), (0, 2, 3))
GROUP = 2
ORDER = [0, 2, 3, 1]
EARLY = (1, 2)


def lane_pick(table, lanes):
    return jnp.take_along_axis(table, lanes, axis=1, mode="promise_in_bounds")


def pick_blocks(blocks, his, los, tracers):
    halves = tracers // 8
    picked = []
    for hi, lo in zip(his, los):
        chains = [[jnp.zeros((8, LANES), jnp.float32)] * 2 for _ in range(halves)]
        for n, (ident, load) in enumerate(blocks):
            hit = hi == ident
            for half in range(halves):
                chain = chains[half]
                chain[n % 2] = jnp.where(hit, lane_pick(load(half), lo), chain[n % 2])
        picked.append([one + two for one, two in chains])
    return picked


def split_pieces(value, pieces, block, tracers):
    top = value.astype(jnp.bfloat16)
    rest = (value - top.astype(jnp.float32)).astype(jnp.bfloat16)
    rows_at = pl.ds(block * tracers, tracers)
    pieces[rows_at, pl.ds(0, LANES)] = top
    pieces[rows_at, pl.ds(LANES, LANES)] = rest


def dot_blocks(left, idents, his, los, tracers):
    halves = tracers // 8
    lane_id = lax.broadcasted_iota(jnp.int32, (LANES, LANES), 0)
    picked = []
    for k in range(0, len(his), PAIR):
        hots = []
        for lo in los[k : k + PAIR]:
            hot = lane_id == jnp.broadcast_to(lo, (LANES, LANES))
            hot = hot.astype(jnp.float32).astype(jnp.bfloat16)
            hots.append(jnp.concatenate([hot, hot], axis=0))
        found = jnp.dot(
            left, jnp.concatenate(hots, axis=1), preferred_element_type=jnp.float32
        )
        for n, hi in enumerate(his[k : k + PAIR]):
            hi = jnp.broadcast_to(hi, (8, LANES))
            part = [jnp.zeros((8, LANES), jnp.float32)] * halves
            for block, ident in enumerate(idents):
                hit = hi == ident
                for half in range(halves):
                    row = block * tracers + half * 8
                    cell = found[row : row + 8, n * LANES : (n + 1) * LANES]
                    part[half] = jnp.where(hit, cell, part[half])
            picked.append(part)
    return picked


def exchange_kernel(
    dims,
    *refs,
):
    sources, refs = refs[:9], refs[9:]
    out_ref, *refs = refs
    (
        lev_ref,
        packed,
        received,
        remapped,
        first,
        pieces,
        surface_pieces,
        pack_send,
        pack_recv,
        field_send,
        field_recv,
        first_send,
        first_recv,
        answer,
        input_sem,
        *staged,
    ) = refs
    (
        tracer_ref,
        vel_ref,
        coup_ref,
        mask_ref,
        rows_ref,
        cols_ref,
        near_ref,
        slot_ref,
        weight_ref,
    ) = staged
    tiles, tracers, levels, rows, chunks, nears, blocks, inters = dims
    groups = rows * chunks
    halves = tracers // 8
    me_c = lax.axis_index("comp")
    me_t = lax.axis_index("tile")
    other = 1 - me_c

    def tile_at(step):
        return lax.rem(me_t + step + tiles, tiles)

    up, down = tile_at(1), tile_at(-1)
    inputs = {}
    for n, (source, ref) in enumerate(zip(sources, staged)):
        inputs[n] = pltpu.make_async_copy(source, ref, input_sem.at[n])
        inputs[n].start()

    links = [(other, 1 - j) for j in range(nears)] + [(me_c, 1), (me_c, -1)]
    barrier = pltpu.get_barrier_semaphore()
    awaited = jnp.int32(0)
    for comp, step in links:
        sends_wrap, takes_wrap = me_t + step < 0, me_t - step >= tiles

        @pl.when(jnp.logical_not(takes_wrap))
        def _(comp=comp, step=step):
            pl.semaphore_signal(
                barrier, inc=1, device_id=(comp, tile_at(-step)), device_id_type=MESH
            )

        @pl.when(sends_wrap)
        def _(comp=comp, step=step):
            pl.semaphore_signal(
                barrier, inc=1, device_id=(comp, tile_at(step)), device_id_type=MESH
            )

        awaited += jnp.where(sends_wrap, 0, 1) + jnp.where(takes_wrap, 1, 0)

    def enter():
        pl.semaphore_wait(barrier, awaited)
        for n, (comp, step) in enumerate(links):

            @pl.when(me_t - step >= tiles)
            def _(n=n, comp=comp, step=step):
                pl.semaphore_signal(
                    answer.at[n],
                    inc=1,
                    device_id=(comp, tile_at(-step)),
                    device_id_type=MESH,
                )

    answers = me_t - min(step for _, step in links) >= tiles
    pl.when(answers)(enter)

    def load_level(level):
        def one(g, _):
            c, r = g // rows, g % rows
            lev_ref[level, 1 + r, c] = tracer_ref[
                pl.ds(level * groups + g, tracers, stride=levels * groups), :
            ]
            return 0

        lax.fori_loop(0, groups, one, 0)

    for n in (0, 4, 5):
        inputs[n].wait()
    load_level(0)

    def wide(ref, row):
        return jnp.broadcast_to(ref[pl.ds(row, 1), :], (8, LANES))

    for r in range(rows):
        for c in range(chunks):
            split_pieces(lev_ref[0, 1 + r, c], surface_pieces, r * chunks + c, tracers)

    def pack(j):
        batch = 16

        def one(b, _):
            his, los = [], []
            for n in range(batch):
                at = (b * batch + n) * nears + j
                row, col = rows_ref[pl.ds(at, 1), :], cols_ref[pl.ds(at, 1), :]
                his.append(row * chunks + (col >> 7))
                los.append(col & 127)
            on_mxu = batch - 6
            picked = dot_blocks(
                surface_pieces[...],
                range(rows * chunks),
                his[:on_mxu],
                los[:on_mxu],
                tracers,
            )
            table = [
                (
                    r * chunks + c,
                    lambda half, r=r, c=c: lev_ref[0, 1 + r, c, pl.ds(half * 8, 8), :],
                )
                for r in range(rows)
                for c in range(chunks)
            ]
            picked += pick_blocks(
                table,
                [jnp.broadcast_to(x, (8, LANES)) for x in his[on_mxu:]],
                [jnp.broadcast_to(x, (8, LANES)) for x in los[on_mxu:]],
                tracers,
            )
            for n in range(batch):
                for half in range(halves):
                    packed[j, b * batch + n, pl.ds(half * 8, 8), :] = picked[n][half]
            return 0

        lax.fori_loop(0, blocks // batch, one, 0)

    late = []

    def start(copy, link):
        step = links[link][1]
        if step >= 0:
            copy.start()
            return
        wraps = me_t + step < 0
        pl.when(jnp.logical_not(wraps))(copy.start)
        late.append((link, wraps, copy))

    def start_late():
        for link in sorted({link for link, _, _ in late}):

            @pl.when(me_t + links[link][1] < 0)
            def _(link=link):
                pl.semaphore_wait(answer.at[link], 1)
                for at, _, copy in late:
                    if at == link:
                        copy.start()

        late.clear()

    order = ORDER
    pack_copies = {}
    for at, j in enumerate(order):
        pack(j)
        if at == 0:
            pl.when(jnp.logical_not(answers))(enter)
        pack_copies[j] = pltpu.make_async_remote_copy(
            src_ref=packed.at[j],
            dst_ref=received.at[j],
            send_sem=pack_send.at[j],
            recv_sem=pack_recv.at[j],
            device_id=(other, tile_at(1 - j)),
            device_id_type=MESH,
        )
        start(pack_copies[j], j)

    def to_side(ref, sends, recvs, level, side):
        src, dst, target = ((1, rows + 1, down), (rows, 0, up))[side]
        copy = pltpu.make_async_remote_copy(
            src_ref=ref.at[level, src],
            dst_ref=ref.at[level, dst],
            send_sem=sends.at[level, side],
            recv_sem=recvs.at[level, side],
            device_id=(me_c, target),
            device_id_type=MESH,
        )
        return copy

    sides = [(level, side) for level in range(levels) for side in (1, 0)]
    field_copies = {at: to_side(lev_ref, field_send, field_recv, *at) for at in sides}
    first_copies = {at: to_side(first, first_send, first_recv, *at) for at in sides}
    for level in range(1, levels):
        load_level(level)
        if level in EARLY:
            for side in (1, 0):
                start(field_copies[level, side], nears + 1 - side)

    for n in (1, 2, 3, 6, 7, 8):
        inputs[n].wait()

    def remap(r, cs, part):
        places = [(j, b) for j in PARTS[part] for b in range(blocks)]
        idents = [j * blocks + b for j, b in places]
        table = [
            (
                j * blocks + b,
                lambda half, j=j, b=b: received[j, b, pl.ds(half * 8, 8), :],
            )
            for j, b in places
        ]
        before = sum(len(js) for js in PARTS[:part]) * blocks * tracers
        left = pieces[pl.ds(before, len(places) * tracers), :]
        his, los, weights = [], [], []
        for c in cs:
            for k in range(inters):
                at = k * groups + c * rows + r
                slot = slot_ref[pl.ds(at, 1), :]
                his.append(near_ref[pl.ds(at, 1), :] * blocks + (slot >> 7))
                los.append(slot & 127)
                weights.append(wide(weight_ref, at))
        on_mxu = len(his) - ON_LANES[part]
        picked = dot_blocks(left, idents, his[:on_mxu], los[:on_mxu], tracers)
        picked += pick_blocks(
            table,
            [jnp.broadcast_to(x, (8, LANES)) for x in his[on_mxu:]],
            [jnp.broadcast_to(x, (8, LANES)) for x in los[on_mxu:]],
            tracers,
        )
        for n, c in enumerate(cs):
            if part == 0:
                sums = [jnp.zeros((8, LANES), jnp.float32)] * halves
            else:
                sums = [remapped[r, c, pl.ds(half * 8, 8), :] for half in range(halves)]
            for k in range(n * inters, (n + 1) * inters):
                sums = [
                    sums[half] + weights[k] * picked[k][half] for half in range(halves)
                ]
            if part == len(PARTS) - 1:
                couple(r, c, sums)
            else:
                for half in range(halves):
                    remapped[r, c, pl.ds(half * 8, 8), :] = sums[half]

    def couple(r, c, sums):
        g = c * rows + r
        mask = wide(mask_ref, g).astype(jnp.float32)
        coup = coup_ref[pl.ds(g, tracers, stride=groups), :]
        for half in range(halves):
            at = pl.ds(half * 8, 8)
            old = lev_ref[0, 1 + r, c, at, :]
            part = coup[half * 8 : half * 8 + 8]
            lev_ref[0, 1 + r, c, at, :] = old + part * mask * (sums[half] - old)

    lane = lax.broadcasted_iota(jnp.int32, (chunks * tracers, LANES), 1)

    def speed(n, row):
        at = n * groups + row
        return jnp.stack(
            [
                jnp.broadcast_to(vel_ref[pl.ds(at + c * rows, 1), :], (tracers, LANES))
                for c in range(chunks)
            ]
        )

    def stepped(ref, level, row):
        west, field, east = ref[level, row], ref[level, row + 1], ref[level, row + 2]
        flat = field.reshape(chunks * tracers, LANES)
        ahead = pltpu.roll(flat, LANES - 1, 1)
        behind = pltpu.roll(flat, 1, 1)
        north = jnp.where(
            lane == LANES - 1,
            jnp.concatenate([ahead[tracers:], ahead[:tracers]], axis=0),
            ahead,
        ).reshape(chunks, tracers, LANES)
        south = jnp.where(
            lane == 0,
            jnp.concatenate([behind[-tracers:], behind[:-tracers]], axis=0),
            behind,
        ).reshape(chunks, tracers, LANES)
        u, v = speed(level, row), speed(levels + level, row)
        return (
            field
            - 0.5 * u * (east - west)
            - 0.5 * v * (north - south)
            + diffusion * (east + west + north + south - 4.0 * field)
        )

    def step_one(level, row):
        first[level, row + 1] = stepped(lev_ref, level, row)

    def step_two(level, row):
        value = stepped(first, level, row)
        for c in range(chunks):
            at = level * groups + c * rows + row
            out_ref[pl.ds(at, tracers, stride=levels * groups), :] = value[c]

    def each_level(start, fn):
        def one(level, _):
            fn(level)
            return 0

        lax.fori_loop(start, levels, one, 0)

    def inside(step, level):
        def one(row, _):
            step(level, row)
            return 0

        lax.fori_loop(1, rows - 1, one, 0)

    def send_field(level, side):
        field_copies[level, side].start()

    def send_first(level, side):
        field_copies[level, 1 - side].wait_recv()
        step_one(level, (0, rows - 1)[side])
        first_copies[level, side].start()

    def gather_row(r, part):
        def one(n, _):
            remap(r, [n * GROUP + i for i in range(GROUP)], part)
            return 0

        lax.fori_loop(0, chunks // GROUP, one, 0, unroll=1)

    def couple_row(r):
        gather_row(r, len(PARTS) - 1)


    def split_slots(place, j):
        def one(b, _):
            split_pieces(received[j, b], pieces, place * blocks + b, tracers)
            return 0

        lax.fori_loop(0, blocks, one, 0)

    inner = list(range(1, levels))
    place = 0
    for part, some in enumerate(PARTS):
        for j in some:
            pack_copies[j].wait_recv()
            split_slots(place, j)
            place += 1
        if part == 0:

            def row_0(i, _):
                gather_row(i, 0)

                @pl.when(i == 0)
                def _():
                    start_late()

                @pl.when(i == 1)
                def _():
                    for level in inner[2:]:
                        for side in (1, 0):
                            send_field(level, side)

                return 0

            lax.fori_loop(0, rows, row_0, 0)

    last = me_t == tiles - 1

    def row_1(i, _):
        gather_row(jnp.where(i == 0, rows - 1, jnp.where(i == 1, 0, rows - i)), 1)

        @pl.when(i == 0)
        def _():
            send_field(0, 1)
            for level in inner[0:1]:
                for side in (1, 0):
                    send_first(level, side)

        @pl.when(i == 1)
        def _():
            send_field(0, 0)
            for level in inner[1:2]:
                for side in (1, 0):
                    send_first(level, side)

        @pl.when((i == 2) & last)
        def _():
            send_first(0, 1)

        @pl.when(i == 2)
        def _():
            for level in inner[2:]:
                for side in (1, 0):
                    send_first(level, side)

        return 0

    lax.fori_loop(0, rows, row_1, 0)
    inside(step_one, 0)
    pl.when(jnp.logical_not(last))(lambda: send_first(0, 1))
    send_first(0, 0)
    each_level(1, lambda level: inside(step_one, level))
    each_level(0, lambda level: inside(step_two, level))
    for level in inner + [0]:
        for side in (1, 0):
            first_copies[level, 1 - side].wait_recv()
            step_two(level, (0, rows - 1)[side])
    for copy in [*pack_copies.values(), *field_copies.values(), *first_copies.values()]:
        copy.wait_send()


def split_rows(x):
    *lead, rows, width = x.shape
    chunks = width // LANES
    x = jnp.swapaxes(x.reshape(*lead, rows, chunks, LANES), -3, -2)
    return x.reshape(-1, LANES)


def per_device(
    tiles,
    tracer,
    velocity,
    coupling,
    sea_mask,
    send_rows,
    send_cols,
    intersection_near,
    intersection_slot,
    intersection_weight,
):
    _, tracers, levels, rows, width = tracer.shape
    nears, capacity = send_rows.shape[2:]
    inters = intersection_slot.shape[1]
    chunks, blocks = width // LANES, capacity // LANES
    dims = (tiles, tracers, levels, rows, chunks, nears, blocks, inters)
    dma = pltpu.SemaphoreType.DMA
    vmem = pl.BlockSpec(memory_space=pltpu.VMEM)
    f32 = jnp.float32
    operands = [
        split_rows(x)
        for x in (
            tracer,
            velocity,
            coupling,
            sea_mask,
            send_rows,
            send_cols,
            intersection_near,
            intersection_slot,
            intersection_weight,
        )
    ]
    out = pl.pallas_call(
        functools.partial(exchange_kernel, dims),
        out_shape=pltpu.VMEM((tracers * levels * rows * chunks, LANES), f32),
        in_specs=[pl.BlockSpec(memory_space=pltpu.HBM)] * 9,
        out_specs=vmem,
        scratch_shapes=[
            pltpu.VMEM((levels, rows + 2, chunks, tracers, LANES), f32),
            pltpu.VMEM((nears, blocks, tracers, LANES), f32),
            pltpu.VMEM((nears, blocks, tracers, LANES), f32),
            pltpu.VMEM((rows, chunks, tracers, LANES), f32),
            pltpu.VMEM((levels, rows + 2, chunks, tracers, LANES), f32),
            pltpu.VMEM((nears * blocks * tracers, 2 * LANES), jnp.bfloat16),
            pltpu.VMEM((rows * chunks * tracers, 2 * LANES), jnp.bfloat16),
            dma((nears,)),
            dma((nears,)),
            dma((levels, 2)),
            dma((levels, 2)),
            dma((levels, 2)),
            dma((levels, 2)),
            pltpu.SemaphoreType.REGULAR((nears + 2,)),
            dma((len(operands),)),
            *[pltpu.VMEM(x.shape, x.dtype) for x in operands],
        ],
        compiler_params=pltpu.CompilerParams(collective_id=0, has_side_effects=True),
    )(*operands)
    out = out.reshape(1, tracers, levels, chunks, rows, LANES)
    return jnp.swapaxes(out, 3, 4).reshape(tracer.shape)


def solution(mesh):
    in_specs = (
        P("comp", None, None, "tile", None),
        P("comp", None, None, "tile", None),
        P("comp", None, "tile", None),
        P("comp", "tile", None),
        P("comp", "tile", None, None),
        P("comp", "tile", None, None),
        P("comp", None, "tile", None),
        P("comp", None, "tile", None),
        P("comp", None, "tile", None),
    )
    out_specs = P("comp", None, None, "tile", None)
    return jax.shard_map(
        functools.partial(per_device, mesh.shape["tile"]),
        mesh=mesh,
        in_specs=in_specs,
        out_specs=out_specs,
        check_vma=False,
    )
```

```python
import functools

import jax
import jax.numpy as jnp
from jax import lax
from jax.experimental import pallas as pl
from jax.experimental.pallas import tpu as pltpu
from jax.sharding import PartitionSpec as P

diffusion = 0.12
LANES = 128
MESH = pl.DeviceIdType.MESH
PAIR = 2
ON_LANES = (6, 6)
PARTS = ((1,), (0, 2, 3))
GROUP = 2
ORDER = [0, 2, 3, 1]
EARLY = ()


def lane_pick(table, lanes):
    return jnp.take_along_axis(table, lanes, axis=1, mode="promise_in_bounds")


def pick_blocks(blocks, his, los, tracers):
    halves = tracers // 8
    picked = []
    for hi, lo in zip(his, los):
        chains = [[jnp.zeros((8, LANES), jnp.float32)] * 2 for _ in range(halves)]
        for n, (ident, load) in enumerate(blocks):
            hit = hi == ident
            for half in range(halves):
                chain = chains[half]
                chain[n % 2] = jnp.where(hit, lane_pick(load(half), lo), chain[n % 2])
        picked.append([one + two for one, two in chains])
    return picked


def split_pieces(value, pieces, block, tracers):
    top = value.astype(jnp.bfloat16)
    rest = (value - top.astype(jnp.float32)).astype(jnp.bfloat16)
    rows_at = pl.ds(block * tracers, tracers)
    pieces[rows_at, pl.ds(0, LANES)] = top
    pieces[rows_at, pl.ds(LANES, LANES)] = rest


def dot_blocks(left, idents, his, los, tracers):
    halves = tracers // 8
    lane_id = lax.broadcasted_iota(jnp.int32, (LANES, LANES), 0)
    picked = []
    for k in range(0, len(his), PAIR):
        hots = []
        for lo in los[k : k + PAIR]:
            hot = lane_id == jnp.broadcast_to(lo, (LANES, LANES))
            hot = hot.astype(jnp.float32).astype(jnp.bfloat16)
            hots.append(jnp.concatenate([hot, hot], axis=0))
        found = jnp.dot(
            left, jnp.concatenate(hots, axis=1), preferred_element_type=jnp.float32
        )
        for n, hi in enumerate(his[k : k + PAIR]):
            hi = jnp.broadcast_to(hi, (8, LANES))
            part = [jnp.zeros((8, LANES), jnp.float32)] * halves
            for block, ident in enumerate(idents):
                hit = hi == ident
                for half in range(halves):
                    row = block * tracers + half * 8
                    cell = found[row : row + 8, n * LANES : (n + 1) * LANES]
                    part[half] = jnp.where(hit, cell, part[half])
            picked.append(part)
    return picked


def exchange_kernel(
    dims,
    *refs,
):
    sources, refs = refs[:9], refs[9:]
    out_ref, *refs = refs
    (
        lev_ref,
        packed,
        received,
        remapped,
        first,
        pieces,
        surface_pieces,
        pack_send,
        pack_recv,
        field_send,
        field_recv,
        first_send,
        first_recv,
        answer,
        input_sem,
        *staged,
    ) = refs
    (
        tracer_ref,
        vel_ref,
        coup_ref,
        mask_ref,
        rows_ref,
        cols_ref,
        near_ref,
        slot_ref,
        weight_ref,
    ) = staged
    tiles, tracers, levels, rows, chunks, nears, blocks, inters = dims
    groups = rows * chunks
    halves = tracers // 8
    me_c = lax.axis_index("comp")
    me_t = lax.axis_index("tile")
    other = 1 - me_c

    def tile_at(step):
        return lax.rem(me_t + step + tiles, tiles)

    up, down = tile_at(1), tile_at(-1)
    inputs = {}
    for n, (source, ref) in enumerate(zip(sources, staged)):
        inputs[n] = pltpu.make_async_copy(source, ref, input_sem.at[n])
        inputs[n].start()

    links = [(other, 1 - j) for j in range(nears)] + [(me_c, 1), (me_c, -1)]
    barrier = pltpu.get_barrier_semaphore()
    awaited = jnp.int32(0)
    for comp, step in links:
        sends_wrap, takes_wrap = me_t + step < 0, me_t - step >= tiles

        @pl.when(jnp.logical_not(takes_wrap))
        def _(comp=comp, step=step):
            pl.semaphore_signal(
                barrier, inc=1, device_id=(comp, tile_at(-step)), device_id_type=MESH
            )

        @pl.when(sends_wrap)
        def _(comp=comp, step=step):
            pl.semaphore_signal(
                barrier, inc=1, device_id=(comp, tile_at(step)), device_id_type=MESH
            )

        awaited += jnp.where(sends_wrap, 0, 1) + jnp.where(takes_wrap, 1, 0)

    def enter():
        pl.semaphore_wait(barrier, awaited)
        for n, (comp, step) in enumerate(links):

            @pl.when(me_t - step >= tiles)
            def _(n=n, comp=comp, step=step):
                pl.semaphore_signal(
                    answer.at[n],
                    inc=1,
                    device_id=(comp, tile_at(-step)),
                    device_id_type=MESH,
                )

    answers = me_t - min(step for _, step in links) >= tiles
    pl.when(answers)(enter)

    def load_level(level):
        def one(g, _):
            c, r = g // rows, g % rows
            lev_ref[level, 1 + r, c] = tracer_ref[
                pl.ds(level * groups + g, tracers, stride=levels * groups), :
            ]
            return 0

        lax.fori_loop(0, groups, one, 0)

    for n in (0, 4, 5):
        inputs[n].wait()
    load_level(0)

    def wide(ref, row):
        return jnp.broadcast_to(ref[pl.ds(row, 1), :], (8, LANES))

    for r in range(rows):
        for c in range(chunks):
            split_pieces(lev_ref[0, 1 + r, c], surface_pieces, r * chunks + c, tracers)

    def pack(j):
        batch = 16

        def one(b, _):
            his, los = [], []
            for n in range(batch):
                at = (b * batch + n) * nears + j
                row, col = rows_ref[pl.ds(at, 1), :], cols_ref[pl.ds(at, 1), :]
                his.append(row * chunks + (col >> 7))
                los.append(col & 127)
            on_mxu = batch - 6
            picked = dot_blocks(
                surface_pieces[...],
                range(rows * chunks),
                his[:on_mxu],
                los[:on_mxu],
                tracers,
            )
            table = [
                (
                    r * chunks + c,
                    lambda half, r=r, c=c: lev_ref[0, 1 + r, c, pl.ds(half * 8, 8), :],
                )
                for r in range(rows)
                for c in range(chunks)
            ]
            picked += pick_blocks(
                table,
                [jnp.broadcast_to(x, (8, LANES)) for x in his[on_mxu:]],
                [jnp.broadcast_to(x, (8, LANES)) for x in los[on_mxu:]],
                tracers,
            )
            for n in range(batch):
                for half in range(halves):
                    packed[j, b * batch + n, pl.ds(half * 8, 8), :] = picked[n][half]
            return 0

        lax.fori_loop(0, blocks // batch, one, 0)

    late = []

    def start(copy, link):
        step = links[link][1]
        if step >= 0:
            copy.start()
            return
        wraps = me_t + step < 0
        pl.when(jnp.logical_not(wraps))(copy.start)
        late.append((link, wraps, copy))

    def start_late():
        for link in [n for n, (_, step) in enumerate(links) if step < 0]:

            @pl.when(me_t + links[link][1] < 0)
            def _(link=link):
                pl.semaphore_wait(answer.at[link], 1)
                for at, _, copy in late:
                    if at == link:
                        copy.start()

        late.clear()

    order = ORDER
    pack_copies = {}
    for at, j in enumerate(order):
        pack(j)
        if at == 0:
            pl.when(jnp.logical_not(answers))(enter)
        pack_copies[j] = pltpu.make_async_remote_copy(
            src_ref=packed.at[j],
            dst_ref=received.at[j],
            send_sem=pack_send.at[j],
            recv_sem=pack_recv.at[j],
            device_id=(other, tile_at(1 - j)),
            device_id_type=MESH,
        )
        start(pack_copies[j], j)

    def to_side(ref, sends, recvs, level, side):
        src, dst, target = ((1, rows + 1, down), (rows, 0, up))[side]
        copy = pltpu.make_async_remote_copy(
            src_ref=ref.at[level, src],
            dst_ref=ref.at[level, dst],
            send_sem=sends.at[level, side],
            recv_sem=recvs.at[level, side],
            device_id=(me_c, target),
            device_id_type=MESH,
        )
        return copy

    sides = [(level, side) for level in range(levels) for side in (1, 0)]
    field_copies = {at: to_side(lev_ref, field_send, field_recv, *at) for at in sides}
    first_copies = {at: to_side(first, first_send, first_recv, *at) for at in sides}
    for level in range(1, levels):
        load_level(level)
        if level in EARLY:
            for side in (1, 0):
                start(field_copies[level, side], nears + 1 - side)

    for n in (1, 2, 3, 6, 7, 8):
        inputs[n].wait()

    def remap(r, cs, part):
        places = [(j, b) for j in PARTS[part] for b in range(blocks)]
        idents = [j * blocks + b for j, b in places]
        table = [
            (
                j * blocks + b,
                lambda half, j=j, b=b: received[j, b, pl.ds(half * 8, 8), :],
            )
            for j, b in places
        ]
        before = sum(len(js) for js in PARTS[:part]) * blocks * tracers
        left = pieces[pl.ds(before, len(places) * tracers), :]
        his, los, weights = [], [], []
        for c in cs:
            for k in range(inters):
                at = k * groups + c * rows + r
                slot = slot_ref[pl.ds(at, 1), :]
                his.append(near_ref[pl.ds(at, 1), :] * blocks + (slot >> 7))
                los.append(slot & 127)
                weights.append(wide(weight_ref, at))
        on_mxu = len(his) - ON_LANES[part]
        picked = dot_blocks(left, idents, his[:on_mxu], los[:on_mxu], tracers)
        picked += pick_blocks(
            table,
            [jnp.broadcast_to(x, (8, LANES)) for x in his[on_mxu:]],
            [jnp.broadcast_to(x, (8, LANES)) for x in los[on_mxu:]],
            tracers,
        )
        for n, c in enumerate(cs):
            if part == 0:
                sums = [jnp.zeros((8, LANES), jnp.float32)] * halves
            else:
                sums = [remapped[r, c, pl.ds(half * 8, 8), :] for half in range(halves)]
            for k in range(n * inters, (n + 1) * inters):
                sums = [
                    sums[half] + weights[k] * picked[k][half] for half in range(halves)
                ]
            if part == len(PARTS) - 1:
                couple(r, c, sums)
            else:
                for half in range(halves):
                    remapped[r, c, pl.ds(half * 8, 8), :] = sums[half]

    def couple(r, c, sums):
        g = c * rows + r
        mask = wide(mask_ref, g).astype(jnp.float32)
        coup = coup_ref[pl.ds(g, tracers, stride=groups), :]
        for half in range(halves):
            at = pl.ds(half * 8, 8)
            old = lev_ref[0, 1 + r, c, at, :]
            part = coup[half * 8 : half * 8 + 8]
            lev_ref[0, 1 + r, c, at, :] = old + part * mask * (sums[half] - old)

    lane = lax.broadcasted_iota(jnp.int32, (chunks * tracers, LANES), 1)

    def speed(n, row):
        at = n * groups + row
        return jnp.stack(
            [
                jnp.broadcast_to(vel_ref[pl.ds(at + c * rows, 1), :], (tracers, LANES))
                for c in range(chunks)
            ]
        )

    def stepped(ref, level, row):
        west, field, east = ref[level, row], ref[level, row + 1], ref[level, row + 2]
        flat = field.reshape(chunks * tracers, LANES)
        ahead = pltpu.roll(flat, LANES - 1, 1)
        behind = pltpu.roll(flat, 1, 1)
        north = jnp.where(
            lane == LANES - 1,
            jnp.concatenate([ahead[tracers:], ahead[:tracers]], axis=0),
            ahead,
        ).reshape(chunks, tracers, LANES)
        south = jnp.where(
            lane == 0,
            jnp.concatenate([behind[-tracers:], behind[:-tracers]], axis=0),
            behind,
        ).reshape(chunks, tracers, LANES)
        u, v = speed(level, row), speed(levels + level, row)
        return (
            field
            - 0.5 * u * (east - west)
            - 0.5 * v * (north - south)
            + diffusion * (east + west + north + south - 4.0 * field)
        )

    def step_one(level, row):
        first[level, row + 1] = stepped(lev_ref, level, row)

    def step_two(level, row):
        value = stepped(first, level, row)
        for c in range(chunks):
            at = level * groups + c * rows + row
            out_ref[pl.ds(at, tracers, stride=levels * groups), :] = value[c]

    def each_level(start, fn):
        def one(level, _):
            fn(level)
            return 0

        lax.fori_loop(start, levels, one, 0)

    def inside(step, level):
        def one(row, _):
            step(level, row)
            return 0

        lax.fori_loop(1, rows - 1, one, 0)

    def send_field(level, side):
        field_copies[level, side].start()

    def send_first(level, side):
        field_copies[level, 1 - side].wait_recv()
        step_one(level, (0, rows - 1)[side])
        first_copies[level, side].start()

    def gather_row(r, part):
        def one(n, _):
            remap(r, [n * GROUP + i for i in range(GROUP)], part)
            return 0

        lax.fori_loop(0, chunks // GROUP, one, 0, unroll=1)

    def couple_row(r):
        gather_row(r, len(PARTS) - 1)


    def split_slots(place, j):
        def one(b, _):
            split_pieces(received[j, b], pieces, place * blocks + b, tracers)
            return 0

        lax.fori_loop(0, blocks, one, 0)

    inner = list(range(1, levels))
    place = 0
    for part, some in enumerate(PARTS):
        for j in some:
            pack_copies[j].wait_recv()
            split_slots(place, j)
            place += 1
        if part == 0:

            ahead = me_t < 2

            def send_fields(some):
                for level in some:
                    for side in (1, 0):
                        send_field(level, side)

            def row_0(i, _):
                gather_row(i, 0)
                pl.when(i == 0)(start_late)
                turn = jnp.where(ahead, i + 1, i)
                pl.when(turn == 1)(lambda: send_fields(inner[:1]))
                pl.when(turn == 2)(lambda: send_fields(inner[1:2]))
                pl.when(turn == 3)(lambda: send_fields(inner[2:]))
                return 0

            lax.fori_loop(0, rows, row_0, 0)

    last = me_t == tiles - 1

    def row_1(i, _):
        gather_row(jnp.where(i == 0, rows - 1, jnp.where(i == 1, 0, rows - i)), 1)

        @pl.when(i == 0)
        def _():
            send_field(0, 1)
            for level in inner[0:1]:
                send_first(level, 1)
                pl.when(me_t > 0)(lambda: send_first(level, 0))

        @pl.when(i == 1)
        def _():
            send_field(0, 0)
            for level in inner[0:1]:
                pl.when(me_t == 0)(lambda: send_first(level, 0))
            for level in inner[1:2]:
                for side in (1, 0):
                    send_first(level, side)

        @pl.when((i == 2) & last)
        def _():
            send_first(0, 1)

        @pl.when(i == 2)
        def _():
            for level in inner[2:]:
                for side in (1, 0):
                    send_first(level, side)

        return 0

    lax.fori_loop(0, rows, row_1, 0)
    inside(step_one, 0)
    pl.when(jnp.logical_not(last))(lambda: send_first(0, 1))
    send_first(0, 0)
    each_level(1, lambda level: inside(step_one, level))
    each_level(0, lambda level: inside(step_two, level))

    def finish(level):
        for side in (1, 0):
            first_copies[level, 1 - side].wait_recv()
            step_two(level, (0, rows - 1)[side])

    for level in inner:
        finish(level)
    inner_firsts = [first_copies[level, side] for level in inner for side in range(2)]
    for copy in [*pack_copies.values(), *field_copies.values(), *inner_firsts]:
        copy.wait_send()
    finish(0)
    for side in range(2):
        first_copies[0, side].wait_send()


def split_rows(x):
    *lead, rows, width = x.shape
    chunks = width // LANES
    x = jnp.swapaxes(x.reshape(*lead, rows, chunks, LANES), -3, -2)
    return x.reshape(-1, LANES)


def per_device(
    tiles,
    tracer,
    velocity,
    coupling,
    sea_mask,
    send_rows,
    send_cols,
    intersection_near,
    intersection_slot,
    intersection_weight,
):
    _, tracers, levels, rows, width = tracer.shape
    nears, capacity = send_rows.shape[2:]
    inters = intersection_slot.shape[1]
    chunks, blocks = width // LANES, capacity // LANES
    dims = (tiles, tracers, levels, rows, chunks, nears, blocks, inters)
    dma = pltpu.SemaphoreType.DMA
    vmem = pl.BlockSpec(memory_space=pltpu.VMEM)
    f32 = jnp.float32
    operands = [
        split_rows(x)
        for x in (
            tracer,
            velocity,
            coupling,
            sea_mask,
            send_rows,
            send_cols,
            intersection_near,
            intersection_slot,
            intersection_weight,
        )
    ]
    out = pl.pallas_call(
        functools.partial(exchange_kernel, dims),
        out_shape=pltpu.VMEM((tracers * levels * rows * chunks, LANES), f32),
        in_specs=[pl.BlockSpec(memory_space=pltpu.HBM)] * 9,
        out_specs=vmem,
        scratch_shapes=[
            pltpu.VMEM((levels, rows + 2, chunks, tracers, LANES), f32),
            pltpu.VMEM((nears, blocks, tracers, LANES), f32),
            pltpu.VMEM((nears, blocks, tracers, LANES), f32),
            pltpu.VMEM((rows, chunks, tracers, LANES), f32),
            pltpu.VMEM((levels, rows + 2, chunks, tracers, LANES), f32),
            pltpu.VMEM((nears * blocks * tracers, 2 * LANES), jnp.bfloat16),
            pltpu.VMEM((rows * chunks * tracers, 2 * LANES), jnp.bfloat16),
            dma((nears,)),
            dma((nears,)),
            dma((levels, 2)),
            dma((levels, 2)),
            dma((levels, 2)),
            dma((levels, 2)),
            pltpu.SemaphoreType.REGULAR((nears + 2,)),
            dma((len(operands),)),
            *[pltpu.VMEM(x.shape, x.dtype) for x in operands],
        ],
        compiler_params=pltpu.CompilerParams(collective_id=0, has_side_effects=True),
    )(*operands)
    out = out.reshape(1, tracers, levels, chunks, rows, LANES)
    return jnp.swapaxes(out, 3, 4).reshape(tracer.shape)


def solution(mesh):
    in_specs = (
        P("comp", None, None, "tile", None),
        P("comp", None, None, "tile", None),
        P("comp", None, "tile", None),
        P("comp", "tile", None),
        P("comp", "tile", None, None),
        P("comp", "tile", None, None),
        P("comp", None, "tile", None),
        P("comp", None, "tile", None),
        P("comp", None, "tile", None),
    )
    out_specs = P("comp", None, None, "tile", None)
    return jax.shard_map(
        functools.partial(per_device, mesh.shape["tile"]),
        mesh=mesh,
        in_specs=in_specs,
        out_specs=out_specs,
        check_vma=False,
    )
```

```python
import functools

import jax
import jax.numpy as jnp
from jax import lax
from jax.experimental import pallas as pl
from jax.experimental.pallas import tpu as pltpu
from jax.sharding import PartitionSpec as P

diffusion = 0.12
LANES = 128
MESH = pl.DeviceIdType.MESH
PAIR = 2
ON_LANES = (6, 6)
PARTS = ((1,), (0, 2, 3))
GROUP = 2
ORDER = [0, 2, 3, 1]
EARLY = ()


def lane_pick(table, lanes):
    return jnp.take_along_axis(table, lanes, axis=1, mode="promise_in_bounds")


def pick_blocks(blocks, his, los, tracers):
    halves = tracers // 8
    picked = []
    for hi, lo in zip(his, los):
        chains = [[jnp.zeros((8, LANES), jnp.float32)] * 2 for _ in range(halves)]
        for n, (ident, load) in enumerate(blocks):
            hit = hi == ident
            for half in range(halves):
                chain = chains[half]
                chain[n % 2] = jnp.where(hit, lane_pick(load(half), lo), chain[n % 2])
        picked.append([one + two for one, two in chains])
    return picked


def split_pieces(value, pieces, block, tracers):
    top = value.astype(jnp.bfloat16)
    rest = (value - top.astype(jnp.float32)).astype(jnp.bfloat16)
    rows_at = pl.ds(block * tracers, tracers)
    pieces[rows_at, pl.ds(0, LANES)] = top
    pieces[rows_at, pl.ds(LANES, LANES)] = rest


def dot_blocks(left, idents, his, los, tracers):
    halves = tracers // 8
    lane_id = lax.broadcasted_iota(jnp.int32, (LANES, LANES), 0)
    picked = []
    for k in range(0, len(his), PAIR):
        hots = []
        for lo in los[k : k + PAIR]:
            hot = lane_id == jnp.broadcast_to(lo, (LANES, LANES))
            hot = hot.astype(jnp.float32).astype(jnp.bfloat16)
            hots.append(jnp.concatenate([hot, hot], axis=0))
        found = jnp.dot(
            left, jnp.concatenate(hots, axis=1), preferred_element_type=jnp.float32
        )
        for n, hi in enumerate(his[k : k + PAIR]):
            hi = jnp.broadcast_to(hi, (8, LANES))
            part = [jnp.zeros((8, LANES), jnp.float32)] * halves
            for block, ident in enumerate(idents):
                hit = hi == ident
                for half in range(halves):
                    row = block * tracers + half * 8
                    cell = found[row : row + 8, n * LANES : (n + 1) * LANES]
                    part[half] = jnp.where(hit, cell, part[half])
            picked.append(part)
    return picked


def exchange_kernel(
    dims,
    *refs,
):
    sources, refs = refs[:9], refs[9:]
    out_ref, *refs = refs
    (
        lev_ref,
        packed,
        received,
        remapped,
        first,
        pieces,
        surface_pieces,
        pack_send,
        pack_recv,
        field_send,
        field_recv,
        first_send,
        first_recv,
        answer,
        input_sem,
        *staged,
    ) = refs
    (
        tracer_ref,
        vel_ref,
        coup_ref,
        mask_ref,
        rows_ref,
        cols_ref,
        near_ref,
        slot_ref,
        weight_ref,
    ) = staged
    tiles, tracers, levels, rows, chunks, nears, blocks, inters = dims
    groups = rows * chunks
    halves = tracers // 8
    me_c = lax.axis_index("comp")
    me_t = lax.axis_index("tile")
    other = 1 - me_c

    def tile_at(step):
        return lax.rem(me_t + step + tiles, tiles)

    up, down = tile_at(1), tile_at(-1)
    inputs = {}
    for n, (source, ref) in enumerate(zip(sources, staged)):
        inputs[n] = pltpu.make_async_copy(source, ref, input_sem.at[n])
        inputs[n].start()

    links = [(other, 1 - j) for j in range(nears)] + [(me_c, 1), (me_c, -1)]
    barrier = pltpu.get_barrier_semaphore()
    awaited = jnp.int32(0)
    for comp, step in links:
        sends_wrap, takes_wrap = me_t + step < 0, me_t - step >= tiles

        @pl.when(jnp.logical_not(takes_wrap))
        def _(comp=comp, step=step):
            pl.semaphore_signal(
                barrier, inc=1, device_id=(comp, tile_at(-step)), device_id_type=MESH
            )

        @pl.when(sends_wrap)
        def _(comp=comp, step=step):
            pl.semaphore_signal(
                barrier, inc=1, device_id=(comp, tile_at(step)), device_id_type=MESH
            )

        awaited += jnp.where(sends_wrap, 0, 1) + jnp.where(takes_wrap, 1, 0)

    def enter():
        pl.semaphore_wait(barrier, awaited)
        for n, (comp, step) in enumerate(links):

            @pl.when(me_t - step >= tiles)
            def _(n=n, comp=comp, step=step):
                pl.semaphore_signal(
                    answer.at[n],
                    inc=1,
                    device_id=(comp, tile_at(-step)),
                    device_id_type=MESH,
                )

    answers = me_t - min(step for _, step in links) >= tiles
    pl.when(answers)(enter)

    def load_level(level):
        def one(g, _):
            c, r = g // rows, g % rows
            lev_ref[level, 1 + r, c] = tracer_ref[
                pl.ds(level * groups + g, tracers, stride=levels * groups), :
            ]
            return 0

        lax.fori_loop(0, groups, one, 0)

    for n in (0, 4, 5):
        inputs[n].wait()
    load_level(0)

    def wide(ref, row):
        return jnp.broadcast_to(ref[pl.ds(row, 1), :], (8, LANES))

    for r in range(rows):
        for c in range(chunks):
            split_pieces(lev_ref[0, 1 + r, c], surface_pieces, r * chunks + c, tracers)

    def pack(j):
        batch = 16

        def one(b, _):
            his, los = [], []
            for n in range(batch):
                at = (b * batch + n) * nears + j
                row, col = rows_ref[pl.ds(at, 1), :], cols_ref[pl.ds(at, 1), :]
                his.append(row * chunks + (col >> 7))
                los.append(col & 127)
            on_mxu = batch - 6
            picked = dot_blocks(
                surface_pieces[...],
                range(rows * chunks),
                his[:on_mxu],
                los[:on_mxu],
                tracers,
            )
            table = [
                (
                    r * chunks + c,
                    lambda half, r=r, c=c: lev_ref[0, 1 + r, c, pl.ds(half * 8, 8), :],
                )
                for r in range(rows)
                for c in range(chunks)
            ]
            picked += pick_blocks(
                table,
                [jnp.broadcast_to(x, (8, LANES)) for x in his[on_mxu:]],
                [jnp.broadcast_to(x, (8, LANES)) for x in los[on_mxu:]],
                tracers,
            )
            for n in range(batch):
                for half in range(halves):
                    packed[j, b * batch + n, pl.ds(half * 8, 8), :] = picked[n][half]
            return 0

        lax.fori_loop(0, blocks // batch, one, 0)

    late = []

    def start(copy, link):
        step = links[link][1]
        if step >= 0:
            copy.start()
            return
        wraps = me_t + step < 0
        pl.when(jnp.logical_not(wraps))(copy.start)
        late.append((link, wraps, copy))

    def start_late():
        for link in [n for n, (_, step) in enumerate(links) if step < 0]:

            @pl.when(me_t + links[link][1] < 0)
            def _(link=link):
                pl.semaphore_wait(answer.at[link], 1)
                for at, _, copy in late:
                    if at == link:
                        copy.start()

        late.clear()

    order = ORDER
    pack_copies = {}
    for at, j in enumerate(order):
        pack(j)
        if at == 0:
            pl.when(jnp.logical_not(answers))(enter)
        pack_copies[j] = pltpu.make_async_remote_copy(
            src_ref=packed.at[j],
            dst_ref=received.at[j],
            send_sem=pack_send.at[j],
            recv_sem=pack_recv.at[j],
            device_id=(other, tile_at(1 - j)),
            device_id_type=MESH,
        )
        start(pack_copies[j], j)

    def to_side(ref, sends, recvs, level, side):
        src, dst, target = ((1, rows + 1, down), (rows, 0, up))[side]
        copy = pltpu.make_async_remote_copy(
            src_ref=ref.at[level, src],
            dst_ref=ref.at[level, dst],
            send_sem=sends.at[level, side],
            recv_sem=recvs.at[level, side],
            device_id=(me_c, target),
            device_id_type=MESH,
        )
        return copy

    sides = [(level, side) for level in range(levels) for side in (1, 0)]
    field_copies = {at: to_side(lev_ref, field_send, field_recv, *at) for at in sides}
    first_copies = {at: to_side(first, first_send, first_recv, *at) for at in sides}
    for level in range(1, levels):
        load_level(level)
        if level in EARLY:
            for side in (1, 0):
                start(field_copies[level, side], nears + 1 - side)

    for n in (1, 2, 3, 6, 7, 8):
        inputs[n].wait()

    def remap(r, cs, part):
        places = [(j, b) for j in PARTS[part] for b in range(blocks)]
        idents = [j * blocks + b for j, b in places]
        table = [
            (
                j * blocks + b,
                lambda half, j=j, b=b: received[j, b, pl.ds(half * 8, 8), :],
            )
            for j, b in places
        ]
        before = sum(len(js) for js in PARTS[:part]) * blocks * tracers
        left = pieces[pl.ds(before, len(places) * tracers), :]
        his, los, weights = [], [], []
        for c in cs:
            for k in range(inters):
                at = k * groups + c * rows + r
                slot = slot_ref[pl.ds(at, 1), :]
                his.append(near_ref[pl.ds(at, 1), :] * blocks + (slot >> 7))
                los.append(slot & 127)
                weights.append(wide(weight_ref, at))
        on_mxu = len(his) - ON_LANES[part]
        picked = dot_blocks(left, idents, his[:on_mxu], los[:on_mxu], tracers)
        picked += pick_blocks(
            table,
            [jnp.broadcast_to(x, (8, LANES)) for x in his[on_mxu:]],
            [jnp.broadcast_to(x, (8, LANES)) for x in los[on_mxu:]],
            tracers,
        )
        for n, c in enumerate(cs):
            if part == 0:
                sums = [jnp.zeros((8, LANES), jnp.float32)] * halves
            else:
                sums = [remapped[r, c, pl.ds(half * 8, 8), :] for half in range(halves)]
            for k in range(n * inters, (n + 1) * inters):
                sums = [
                    sums[half] + weights[k] * picked[k][half] for half in range(halves)
                ]
            if part == len(PARTS) - 1:
                couple(r, c, sums)
            else:
                for half in range(halves):
                    remapped[r, c, pl.ds(half * 8, 8), :] = sums[half]

    def couple(r, c, sums):
        g = c * rows + r
        mask = wide(mask_ref, g).astype(jnp.float32)
        coup = coup_ref[pl.ds(g, tracers, stride=groups), :]
        for half in range(halves):
            at = pl.ds(half * 8, 8)
            old = lev_ref[0, 1 + r, c, at, :]
            part = coup[half * 8 : half * 8 + 8]
            lev_ref[0, 1 + r, c, at, :] = old + part * mask * (sums[half] - old)

    lane = lax.broadcasted_iota(jnp.int32, (chunks * tracers, LANES), 1)

    def speed(n, row):
        at = n * groups + row
        return jnp.stack(
            [
                jnp.broadcast_to(vel_ref[pl.ds(at + c * rows, 1), :], (tracers, LANES))
                for c in range(chunks)
            ]
        )

    def stepped(ref, level, row):
        west, field, east = ref[level, row], ref[level, row + 1], ref[level, row + 2]
        flat = field.reshape(chunks * tracers, LANES)
        ahead = pltpu.roll(flat, LANES - 1, 1)
        behind = pltpu.roll(flat, 1, 1)
        north = jnp.where(
            lane == LANES - 1,
            jnp.concatenate([ahead[tracers:], ahead[:tracers]], axis=0),
            ahead,
        ).reshape(chunks, tracers, LANES)
        south = jnp.where(
            lane == 0,
            jnp.concatenate([behind[-tracers:], behind[:-tracers]], axis=0),
            behind,
        ).reshape(chunks, tracers, LANES)
        u, v = speed(level, row), speed(levels + level, row)
        return (
            field
            - 0.5 * u * (east - west)
            - 0.5 * v * (north - south)
            + diffusion * (east + west + north + south - 4.0 * field)
        )

    def step_one(level, row):
        first[level, row + 1] = stepped(lev_ref, level, row)

    def step_two(level, row):
        value = stepped(first, level, row)
        for c in range(chunks):
            at = level * groups + c * rows + row
            out_ref[pl.ds(at, tracers, stride=levels * groups), :] = value[c]

    def each_level(start, fn):
        def one(level, _):
            fn(level)
            return 0

        lax.fori_loop(start, levels, one, 0)

    def inside(step, level):
        def one(row, _):
            step(level, row)
            return 0

        lax.fori_loop(1, rows - 1, one, 0)

    def send_field(level, side):
        field_copies[level, side].start()

    def send_first(level, side):
        field_copies[level, 1 - side].wait_recv()
        step_one(level, (0, rows - 1)[side])
        first_copies[level, side].start()

    def gather_row(r, part):
        def one(n, _):
            remap(r, [n * GROUP + i for i in range(GROUP)], part)
            return 0

        lax.fori_loop(0, chunks // GROUP, one, 0, unroll=1)

    def couple_row(r):
        gather_row(r, len(PARTS) - 1)


    def split_slots(place, j):
        def one(b, _):
            split_pieces(received[j, b], pieces, place * blocks + b, tracers)
            return 0

        lax.fori_loop(0, blocks, one, 0)

    inner = list(range(1, levels))
    place = 0
    for part, some in enumerate(PARTS):
        for j in some:
            pack_copies[j].wait_recv()
            split_slots(place, j)
            place += 1
        if part == 0:

            ahead = me_t < 2

            def send_fields(some):
                for level in some:
                    for side in (1, 0):
                        send_field(level, side)

            def row_0(i, _):
                gather_row(i, 0)
                pl.when(i == 0)(start_late)
                turn = jnp.where(ahead, i + 1, i)
                pl.when(turn == 1)(lambda: send_fields(inner[:1]))
                pl.when(turn == 2)(lambda: send_fields(inner[1:2]))
                pl.when(turn == 3)(lambda: send_fields(inner[2:]))
                return 0

            lax.fori_loop(0, rows, row_0, 0)

    last = me_t == tiles - 1

    def row_1(i, _):
        gather_row(jnp.where(i == 0, rows - 1, jnp.where(i == 1, 0, rows - i)), 1)

        @pl.when(i == 0)
        def _():
            send_field(0, 1)
            for level in inner[0:1]:
                send_first(level, 1)
                pl.when(me_t > 0)(lambda: send_first(level, 0))

        @pl.when(i == 1)
        def _():
            send_field(0, 0)
            for level in inner[0:1]:
                pl.when(me_t == 0)(lambda: send_first(level, 0))
            for level in inner[1:2]:
                for side in (1, 0):
                    send_first(level, side)

        @pl.when((i == 2) & last)
        def _():
            send_first(0, 1)

        @pl.when(i == 2)
        def _():
            for level in inner[2:]:
                for side in (1, 0):
                    send_first(level, side)

        return 0

    lax.fori_loop(0, rows, row_1, 0)
    inside(step_one, 0)
    send_first(0, 0)
    pl.when(jnp.logical_not(last))(lambda: send_first(0, 1))
    each_level(1, lambda level: inside(step_one, level))
    each_level(0, lambda level: inside(step_two, level))

    def finish(level):
        for side in (1, 0):
            first_copies[level, 1 - side].wait_recv()
            step_two(level, (0, rows - 1)[side])

    for level in inner:
        finish(level)
    inner_firsts = [first_copies[level, side] for level in inner for side in range(2)]
    for copy in [*pack_copies.values(), *field_copies.values(), *inner_firsts]:
        copy.wait_send()
    finish(0)
    for side in range(2):
        first_copies[0, side].wait_send()


def split_rows(x):
    *lead, rows, width = x.shape
    chunks = width // LANES
    x = jnp.swapaxes(x.reshape(*lead, rows, chunks, LANES), -3, -2)
    return x.reshape(-1, LANES)


def per_device(
    tiles,
    tracer,
    velocity,
    coupling,
    sea_mask,
    send_rows,
    send_cols,
    intersection_near,
    intersection_slot,
    intersection_weight,
):
    _, tracers, levels, rows, width = tracer.shape
    nears, capacity = send_rows.shape[2:]
    inters = intersection_slot.shape[1]
    chunks, blocks = width // LANES, capacity // LANES
    dims = (tiles, tracers, levels, rows, chunks, nears, blocks, inters)
    dma = pltpu.SemaphoreType.DMA
    vmem = pl.BlockSpec(memory_space=pltpu.VMEM)
    f32 = jnp.float32
    operands = [
        split_rows(x)
        for x in (
            tracer,
            velocity,
            coupling,
            sea_mask,
            send_rows,
            send_cols,
            intersection_near,
            intersection_slot,
            intersection_weight,
        )
    ]
    out = pl.pallas_call(
        functools.partial(exchange_kernel, dims),
        out_shape=pltpu.VMEM((tracers * levels * rows * chunks, LANES), f32),
        in_specs=[pl.BlockSpec(memory_space=pltpu.HBM)] * 9,
        out_specs=vmem,
        scratch_shapes=[
            pltpu.VMEM((levels, rows + 2, chunks, tracers, LANES), f32),
            pltpu.VMEM((nears, blocks, tracers, LANES), f32),
            pltpu.VMEM((nears, blocks, tracers, LANES), f32),
            pltpu.VMEM((rows, chunks, tracers, LANES), f32),
            pltpu.VMEM((levels, rows + 2, chunks, tracers, LANES), f32),
            pltpu.VMEM((nears * blocks * tracers, 2 * LANES), jnp.bfloat16),
            pltpu.VMEM((rows * chunks * tracers, 2 * LANES), jnp.bfloat16),
            dma((nears,)),
            dma((nears,)),
            dma((levels, 2)),
            dma((levels, 2)),
            dma((levels, 2)),
            dma((levels, 2)),
            pltpu.SemaphoreType.REGULAR((nears + 2,)),
            dma((len(operands),)),
            *[pltpu.VMEM(x.shape, x.dtype) for x in operands],
        ],
        compiler_params=pltpu.CompilerParams(collective_id=0, has_side_effects=True),
    )(*operands)
    out = out.reshape(1, tracers, levels, chunks, rows, LANES)
    return jnp.swapaxes(out, 3, 4).reshape(tracer.shape)


def solution(mesh):
    in_specs = (
        P("comp", None, None, "tile", None),
        P("comp", None, None, "tile", None),
        P("comp", None, "tile", None),
        P("comp", "tile", None),
        P("comp", "tile", None, None),
        P("comp", "tile", None, None),
        P("comp", None, "tile", None),
        P("comp", None, "tile", None),
        P("comp", None, "tile", None),
    )
    out_specs = P("comp", None, None, "tile", None)
    return jax.shard_map(
        functools.partial(per_device, mesh.shape["tile"]),
        mesh=mesh,
        in_specs=in_specs,
        out_specs=out_specs,
        check_vma=False,
    )
```
